256 devices in a mesh: mode: 8 (over x, core), body: 32 (over y, z).
Axes of the slice: x: 4, y: 4, z: 8, core: 2. Of those that a mesh axis runs over, the one named last changes fastest.
Arguments:
- incident: bfloat16 [32, 32, 2, 8, 512], P('body', 'mode'), may hold values from -6 to 6
- inverse: bfloat16 [32, 32, 2, 512, 512], P('body', 'mode'), may hold values from -0.1875 to 0.1875
- coupling: bfloat16 [32, 2, 512, 384], P('body'), may hold values from -0.21875 to 0.21875
- cycle_weight: bfloat16 [32, 256, 384], P('body', 'mode'), may hold values from 0.5 to 4
- near_bodies: int32 [32, 6], replicated, may hold values from 0 to 31, as said below
- cycle_nodes: int32 [32, 6, 64], replicated, may hold values from 0 to 511
- cycle_counts: int32 [32, 6], replicated, may hold values from 1 to 64, as said below
Outputs:
- density: bfloat16 [32, 32, 2, 8, 512], P('body', 'mode')
The draws below stay inside these ranges and needn't reach their ends.
Inputs may be any that keep to these rules, and one draw needn't show every extreme that they name: `near_bodies`: each row lists 6 different bodies, none equal to the row's own index. `cycle_nodes`: entries past a slot's live count are drawn as well and are not used. Only the first cycle_counts[t, n] entries of cycle_nodes[t, n] are live; in every draw some entry of cycle_counts equals 64.
All inputs are finite; a program needn't handle non-finite values.
Results may differ from the reference program's by a relative error of at most 0.022.
Values may be sent and summed in bfloat16 or wider, within the bound.
A program may use at most 128 MiB of HBM per device.

```python
import math
import jax
import jax.numpy as jnp
from jax import lax

P_SIZE = 512
MODES = 32
NA = 256
INC = 8
NB = 6
CAP = 64
ITERS = 2
SLOTS = 384
BODIES = 32


def draw_near_bodies(key, part):
    row_keys = jax.random.split(jax.random.fold_in(key, 11), BODIES)
    offsets = jax.vmap(lambda row_key: jax.random.permutation(row_key, BODIES - 1)[:NB])(row_keys)
    rows_index = jnp.arange(BODIES, dtype=jnp.int32)[:, None]
    return ((rows_index + 1 + offsets.astype(jnp.int32)) % BODIES).astype(jnp.int32)


def draw_cycle_counts(key, part):
    first_key, second_key = jax.random.split(jax.random.fold_in(key, 23))
    counts = jax.random.randint(first_key, (BODIES, NB), 1, CAP + 1, dtype=jnp.int32)
    chosen_spot = jax.random.randint(second_key, (), 0, BODIES * NB, dtype=jnp.int32)
    flat_counts = jnp.where(jnp.arange(BODIES * NB, dtype=jnp.int32) == chosen_spot, CAP, counts.reshape(-1))
    return flat_counts.reshape(BODIES, NB).astype(jnp.int32)


def plant(drawn, key, least, high):
    extent = drawn.shape
    place = [jax.random.randint(jax.random.fold_in(key, axis), (), 0, extent[axis]) for axis in range(len(extent))]
    drawn = drawn.at[tuple(place)].set(least)
    longest = extent.index(max(extent))
    place[longest] = (place[longest] + 1) % extent[longest]
    return drawn.at[tuple(place)].set(high)


def levels(own_key, shape, cuts, low, top_value):
    gain, own = 1.0, jax.random.fold_in(own_key, 6)
    for dim, shards_of in cuts:
        draws = jnp.exp(jax.random.uniform(jax.random.fold_in(own, dim), (shards_of,), jnp.float32, low / len(cuts), top_value / len(cuts)))
        gain = gain * jnp.repeat(draws, shape[dim] // shards_of).reshape([-1 if axis == dim else 1 for axis in range(len(shape))])
    return gain


def centred(rng, shape, scale, reach, shards=(), held_as=jnp.bfloat16):
    drawn = scale * jax.random.normal(rng, shape, jnp.float32)
    if shards:
        drawn = drawn * levels(rng, shape, shards, -0.22, 0.18)
    return jnp.clip(drawn, -reach, reach).astype(held_as)


def setup_inputs(seed: int = 0) -> dict:
    keys = jax.random.split(jax.random.key(seed), 8)
    return {
        "incident": centred(keys[0], (BODIES, MODES, 2, INC, P_SIZE), 1.0, 6.0, ((0, 32), (1, 8))),
        "inverse": centred(keys[1], (BODIES, MODES, 2, P_SIZE, P_SIZE), (2 * P_SIZE) ** -0.5, 0.1875, ((0, 32), (1, 8))),
        "coupling": centred(keys[2], (BODIES, 2, P_SIZE, SLOTS), (2 * SLOTS) ** -0.5, 0.21875, ((0, 32),)),
        "cycle_weight": jnp.clip(jnp.exp(math.log(4.0) - 2.0794415 * jax.random.uniform(keys[3], (BODIES, NA, SLOTS), jnp.float32) ** levels(keys[3], (BODIES, NA, SLOTS), ((0, 32), (1, 8)), -0.2, 0.2)), 0.5, 4.0).astype(jnp.bfloat16),
        "near_bodies": draw_near_bodies(jax.random.fold_in(keys[7], 71), 0),
        "cycle_nodes": plant(jax.random.randint(keys[5], (BODIES, NB, CAP), 0, P_SIZE), jax.random.fold_in(keys[5], 1), 0, P_SIZE - 1).astype(jnp.int32),
        "cycle_counts": draw_cycle_counts(jax.random.fold_in(keys[7], 71), 0),
    }


def wave_values(first_mode, count_modes, first_angle, count_angles):
    wavenum = first_mode + jnp.arange(count_modes, dtype=jnp.int32) - MODES // 2
    angle_index = first_angle + jnp.arange(count_angles, dtype=jnp.int32)
    residue = (wavenum[:, None] * angle_index[None, :]) % NA
    theta_values = residue.astype(jnp.float32) * (2.0 * math.pi / NA)
    return jnp.cos(theta_values), jnp.sin(theta_values)


def upward_table(cosine_part, sine_part):
    return jnp.stack([jnp.stack([cosine_part, sine_part], -1), jnp.stack([-sine_part, cosine_part], -1)], 1).astype(jnp.bfloat16)


def downward_table(cosine_part, sine_part):
    flip_cos = cosine_part.T
    flip_sin = sine_part.T
    return jnp.stack([jnp.stack([flip_cos, -flip_sin], -1), jnp.stack([flip_sin, flip_cos], -1)], 1).astype(jnp.bfloat16)


def apply_inverse(inverse_blocks, right_side):
    product = jnp.einsum('mcqp,mdip->mcdiq', inverse_blocks.astype(jnp.float32), right_side.astype(jnp.float32), precision=lax.Precision.HIGHEST)
    real_part = product[:, 0, 0] - product[:, 1, 1]
    imag_part = product[:, 1, 0] + product[:, 0, 1]
    return jnp.stack([real_part, imag_part], 1).astype(jnp.bfloat16)


def reference(incident, inverse, coupling, cycle_weight, near_bodies, cycle_nodes, cycle_counts):
    cosine_all, sine_all = wave_values(0, MODES, 0, NA)
    upward = upward_table(cosine_all, sine_all).astype(jnp.float32)
    downward = downward_table(cosine_all, sine_all).astype(jnp.float32)
    density = lax.map(lambda operands: apply_inverse(operands[0], operands[1]), (inverse, incident))
    live_slots = jnp.arange(CAP, dtype=jnp.int32)[None, None, :] < cycle_counts[:, :, None]

    def one_body(body_items):
        cycle_modal, weights, couple, source_side, inverse_blocks = body_items
        upsampled = jnp.einsum('jkci,kcad->jadi', cycle_modal.astype(jnp.float32), upward, precision=lax.Precision.HIGHEST).astype(jnp.bfloat16)
        scaled = (upsampled.astype(jnp.float32) * weights.T.astype(jnp.float32)[:, :, None, None]).astype(jnp.bfloat16)
        stacked = scaled.reshape(SLOTS, NA * 2 * INC)
        real_rows = jnp.dot(couple[0], stacked, preferred_element_type=jnp.float32).reshape(P_SIZE, NA, 2, INC)
        imag_rows = jnp.dot(couple[1], stacked, preferred_element_type=jnp.float32).reshape(P_SIZE, NA, 2, INC)
        near_field = jnp.stack([real_rows[:, :, 0] - imag_rows[:, :, 1], imag_rows[:, :, 0] + real_rows[:, :, 1]], 2)
        correction = jnp.einsum('qadi,adkc->kciq', near_field, downward, precision=lax.Precision.HIGHEST)
        residual_side = (source_side.astype(jnp.float32) - correction * (1.0 / NA)).astype(jnp.bfloat16)
        return apply_inverse(inverse_blocks, residual_side)

    for iteration in range(ITERS):
        gathered = density[near_bodies[:, :, None], :, :, :, cycle_nodes]
        gathered = jnp.where(live_slots[:, :, :, None, None, None], gathered, 0)
        gathered = gathered.reshape(BODIES, SLOTS, MODES, 2, INC)
        density = lax.map(one_body, (gathered, cycle_weight, coupling, incident, inverse))
    return density
```

```python
import math

import jax
import jax.numpy as jnp
import numpy as np
from jax import lax
from jax.experimental import pallas as pl
from jax.experimental.pallas import tpu as pltpu
from jax.sharding import PartitionSpec as P

MODES = 32
NA = 256
ITERS = 2
ZDIM = 8
MESH = pl.DeviceIdType.MESH
BF = jnp.bfloat16
F32 = jnp.float32


def tables():
    wavenum = np.arange(MODES) - MODES // 2
    residue = (wavenum[:, None] * np.arange(NA)[None, :]) % NA
    theta = residue.astype(np.float32) * np.float32(2.0 * math.pi / NA)
    cos, sin = np.cos(theta), np.sin(theta)
    up = np.stack([np.stack([cos, sin], -1), np.stack([-sin, cos], -1)], 1)
    up = up.transpose(3, 2, 0, 1).reshape(2 * NA, 2 * MODES)
    down = np.stack([np.stack([cos, sin], 1), np.stack([-sin, cos], 1)], 1)
    turned = np.stack([-down[:, 1], down[:, 0]], 1)
    down = np.concatenate([down.reshape(2 * MODES, 2 * NA), turned.reshape(2 * MODES, 2 * NA)], 0)
    return up.astype(BF), down.astype(BF)


def offsets(bodies):
    ydim = bodies // ZDIM
    far = lambda d, n: min(d, n - d)
    order = [(dy, dz) for dy in range(ydim) for dz in range(ZDIM)]
    order.sort(key=lambda o: (-far(o[1], ZDIM), -far(o[0], ydim), o))
    return order


def target(body, dy, dz, ydim):
    return lax.rem(body // ZDIM + dy, ydim) * ZDIM + lax.rem(lax.rem(body, ZDIM) + dz, ZDIM)


def dot_nt(left, right):
    return lax.dot_general(left, right, (((1,), (1,)), ((), ())), preferred_element_type=F32)


def kernel(
    n_mode, n_body, near_ref, nodes_ref, up_ref, down_ref, inc_ref, w_ref, inv_hbm, coup_hbm, out_ref,
    inv_v, coup_v, onehot, dens, snd1, recv1a, recv1b, gbuf, snd2, recv2, snd3, recv3, rbuf, wall,
    load_sem, send_sem, recv_sem,
):
    me = lax.axis_index("mode")
    body = lax.axis_index("body")
    ydim = n_body // ZDIM
    modes = inv_v.shape[0]
    near = near_ref.shape[1]
    cap = 64
    tiles = rbuf.shape[0]

    loads = [pltpu.make_async_copy(inv_hbm.at[k], inv_v.at[k], load_sem.at[k]) for k in range(modes)]
    loads.append(pltpu.make_async_copy(coup_hbm, coup_v, load_sem.at[modes]))
    for load in loads:
        load.start()

    barrier = pltpu.get_barrier_semaphore()

    @pl.loop(1, n_body)
    def _(off):
        pl.semaphore_signal(
            barrier, inc=1, device_id={"body": lax.rem(body + off, n_body)}, device_id_type=MESH
        )

    @pl.loop(1, n_mode)
    def _(off):
        pl.semaphore_signal(
            barrier, inc=1, device_id={"mode": lax.rem(me + off, n_mode)}, device_id_type=MESH
        )

    groups = onehot.shape[0]
    width = onehot.shape[2]
    node_index = lax.broadcasted_iota(jnp.int32, onehot.shape[1:], 0)
    for g in range(groups):
        row = nodes_ref[:, g * width : (g + 1) * width]
        onehot[g] = jnp.where(node_index == row, 1.0, 0.0).astype(BF)

    def to_modes(src, dst, slot):
        @pl.loop(1, n_mode)
        def _(off):
            peer = lax.rem(me + off, n_mode)
            pltpu.make_async_remote_copy(
                src_ref=src.at[peer], dst_ref=dst.at[me], send_sem=send_sem.at[slot],
                recv_sem=recv_sem.at[slot], device_id={"mode": peer}, device_id_type=MESH,
            ).start()

        pltpu.make_async_copy(src.at[me], dst.at[me], recv_sem.at[slot]).start()

    def arrived(dst, slot):
        pltpu.make_async_copy(dst, dst, recv_sem.at[slot]).wait()

    def sent(src, slot, count):
        part = src.at[pl.ds(0, count)]
        pltpu.make_async_copy(part, part, send_sem.at[slot]).wait()

    lane = lax.broadcasted_iota(jnp.int32, (32, 128), 1)
    low = lane < cap

    def inverse_product(k, real, imag):
        first = jnp.concatenate([real, imag], 0).astype(BF)
        second = jnp.concatenate([-imag, real], 0).astype(BF)
        return dot_nt(first, inv_v[k, 0]) + dot_nt(second, inv_v[k, 1])

    for k in range(modes):
        loads[k].wait()
        value = inverse_product(k, inc_ref[k, 0].astype(F32), inc_ref[k, 1].astype(F32))
        dens[16 * k : 16 * k + 16] = value.astype(BF)

    pl.semaphore_wait(barrier, n_body + n_mode - 2)

    @pl.loop(1, n_mode)
    def _(off):
        pltpu.make_async_remote_copy(
            src_ref=w_ref, dst_ref=wall.at[me], send_sem=send_sem.at[6], recv_sem=recv_sem.at[6],
            device_id={"mode": lax.rem(me + off, n_mode)}, device_id_type=MESH,
        ).start()

    pltpu.make_async_copy(w_ref, wall.at[me], recv_sem.at[6]).start()

    order = offsets(n_body)
    per_group = width // cap
    for it in range(ITERS):
        to_body, from_body = snd1.at[it], (recv1a, recv1b)[it]

        def send_group(g, it=it, to_body=to_body, from_body=from_body):
            for r in range(g * per_group, (g + 1) * per_group):
                if r == n_body - 1:
                    pltpu.make_async_copy(to_body.at[r], from_body.at[body], recv_sem.at[3 * it]).start()
                else:
                    pltpu.make_async_remote_copy(
                        src_ref=to_body.at[r], dst_ref=from_body.at[body], send_sem=send_sem.at[3 * it],
                        recv_sem=recv_sem.at[3 * it],
                        device_id={"body": target(body, *order[r], ydim)}, device_id_type=MESH,
                    ).start()

        all_dens = dens[...]
        for g in range(groups):
            picked = jnp.dot(all_dens, onehot[g], preferred_element_type=F32)
            for pair in range(per_group // 2):
                part = picked[:, 128 * pair : 128 * pair + 128]
                top, bottom = part[:32], part[32:]
                r = g * per_group + 2 * pair
                snd1[it, r] = jnp.where(low, top, pltpu.roll(bottom, cap, 1)).astype(BF)
                snd1[it, r + 1] = jnp.where(low, pltpu.roll(top, cap, 1), bottom).astype(BF)
            if g > 0:
                send_group(g - 1)
        send_group(groups - 1)

        arrived(from_body, 3 * it)
        for v in range(near // 2):
            a = from_body[near_ref[body, 2 * v]].astype(F32)
            b = from_body[near_ref[body, 2 * v + 1]].astype(F32)
            gbuf[v, 0:32] = jnp.where(low, a, pltpu.roll(b, cap, 1))
            gbuf[v, 32:64] = jnp.where(low, pltpu.roll(a, cap, 1), b)
        for i in range(n_mode):
            picked = [gbuf[v, pl.ds(i, 8, stride=8), :] for v in range(near // 2)]
            snd2[it, i] = jnp.concatenate(picked, 1).astype(BF)
        to_modes(snd2.at[it], recv2.at[it], 3 * it + 1)
        arrived(recv2.at[it], 3 * it + 1)

        modal = jnp.concatenate([recv2[it, j].astype(F32) for j in range(n_mode)], 0).astype(BF)
        cycles = jnp.dot(up_ref[...], modal, preferred_element_type=F32)
        if it == 0:
            arrived(wall, 6)
            loads[modes].wait()
        weights = wall[...].astype(F32).reshape(NA, -1)
        scaled = jnp.concatenate([cycles[:NA] * weights, cycles[NA:] * weights], 0).astype(BF)
        back = jnp.dot(down_ref[...], scaled, preferred_element_type=F32).astype(BF)
        half = back.shape[0] // 2
        correction = dot_nt(back[:half], coup_v[0]) + dot_nt(back[half:], coup_v[1])
        for j in range(n_mode):
            snd3[it, j] = correction[8 * j : 8 * j + 8].astype(BF)
        to_modes(snd3.at[it], recv3.at[it], 3 * it + 2)
        arrived(recv3.at[it], 3 * it + 2)

        for i in range(n_mode):
            value = recv3[it, i].astype(F32)
            for q in range(tiles):
                rbuf[q, 8 * i : 8 * i + 8] = value[:, 128 * q : 128 * q + 128]
        for k in range(modes):
            sides = []
            for c in range(2):
                value = [rbuf[q, pl.ds(2 * k + c, 8, stride=8), :] for q in range(tiles)]
                value = jnp.concatenate(value, 1)
                sides.append(inc_ref[k, c].astype(F32) - value * (1.0 / NA))
            value = inverse_product(k, *sides).astype(BF)
            if it < ITERS - 1:
                dens[16 * k : 16 * k + 16] = value
            else:
                out_ref[16 * k : 16 * k + 16] = value

    for it in range(ITERS):
        sent(snd1.at[it], 3 * it, n_body - 1)
        sent(snd2.at[it], 3 * it + 1, n_mode - 1)
        sent(snd3.at[it], 3 * it + 2, n_mode - 1)
    sent(wall, 6, n_mode - 1)


def solution(mesh):
    n_mode, n_body = mesh.shape["mode"], mesh.shape["body"]
    up, down = tables()
    dy, dz = (np.array(x, np.int32) for x in zip(*offsets(n_body)))

    def local(incident, inverse, coupling, cycle_weight, near_bodies, cycle_nodes, cycle_counts):
        body = lax.axis_index("body")
        bodies, near = near_bodies.shape
        cap = cycle_nodes.shape[2]
        modes, inc, nodes = incident.shape[1], incident.shape[3], incident.shape[4]
        slots = near * cap
        listed = near_bodies == body
        send_nodes = jnp.sum(jnp.where(listed[:, :, None], cycle_nodes, 0), axis=1)
        send_counts = jnp.sum(jnp.where(listed, cycle_counts, 0), axis=1)
        live = jnp.arange(cap, dtype=jnp.int32)[None, :] < send_counts[:, None]
        send_nodes = jnp.where(live, send_nodes, -1)
        order = target(body, jnp.asarray(dy), jnp.asarray(dz), bodies // ZDIM)
        node_row = send_nodes[order].reshape(1, bodies * cap)
        rows = modes * 2 * inc
        width = 256
        vmem = pl.BlockSpec(memory_space=pltpu.VMEM)
        hbm = pl.BlockSpec(memory_space=pl.ANY)
        out = pl.pallas_call(
            lambda *refs: kernel(n_mode, n_body, *refs),
            out_shape=jax.ShapeDtypeStruct((rows, nodes), BF),
            in_specs=[pl.BlockSpec(memory_space=pltpu.SMEM), vmem, vmem, vmem, vmem, vmem, hbm, hbm],
            out_specs=vmem,
            scratch_shapes=[
                pltpu.VMEM((modes, 2, nodes, nodes), BF),
                pltpu.VMEM((2, nodes, slots), BF),
                pltpu.VMEM((bodies * cap // width, nodes, width), BF),
                pltpu.VMEM((rows, nodes), BF),
                pltpu.VMEM((ITERS, bodies, rows // 2, 2 * cap), BF),
                pltpu.VMEM((bodies, rows // 2, 2 * cap), BF),
                pltpu.VMEM((bodies, rows // 2, 2 * cap), BF),
                pltpu.VMEM((slots // 128, rows, 128), F32),
                pltpu.VMEM((ITERS, n_mode, 2 * modes, slots), BF),
                pltpu.VMEM((ITERS, n_mode, 2 * modes, slots), BF),
                pltpu.VMEM((ITERS, n_mode, 2 * modes, nodes), BF),
                pltpu.VMEM((ITERS, n_mode, 2 * modes, nodes), BF),
                pltpu.VMEM((nodes // 128, rows, 128), F32),
                pltpu.VMEM((n_mode, NA // n_mode, slots), BF),
                pltpu.SemaphoreType.DMA((modes + 1,)),
                pltpu.SemaphoreType.DMA((3 * ITERS + 1,)),
                pltpu.SemaphoreType.DMA((3 * ITERS + 1,)),
            ],
            compiler_params=pltpu.CompilerParams(collective_id=0, has_side_effects=True),
            name="sweeps",
        )(
            near_bodies, node_row, jnp.asarray(up), jnp.asarray(down), incident[0], cycle_weight[0],
            inverse[0], coupling[0],
        )
        return out.reshape(1, modes, 2, inc, nodes)

    in_specs = (
        P("body", "mode", None, None, None),
        P("body", "mode", None, None, None),
        P("body", None, None, None),
        P("body", "mode", None),
        P(),
        P(),
        P(),
    )
    out_specs = P("body", "mode", None, None, None)
    return jax.shard_map(local, mesh=mesh, in_specs=in_specs, out_specs=out_specs, check_vma=False)
```

```python
import math

import jax
import jax.numpy as jnp
import numpy as np
from jax import lax
from jax.experimental import pallas as pl
from jax.experimental.pallas import tpu as pltpu
from jax.sharding import PartitionSpec as P

MODES = 32
NA = 256
ITERS = 2
ZDIM = 8
MESH = pl.DeviceIdType.MESH
BF = jnp.bfloat16
F32 = jnp.float32


def tables():
    wavenum = np.arange(MODES) - MODES // 2
    residue = (wavenum[:, None] * np.arange(NA)[None, :]) % NA
    theta = residue.astype(np.float32) * np.float32(2.0 * math.pi / NA)
    cos, sin = np.cos(theta), np.sin(theta)
    up = np.stack([np.stack([cos, sin], -1), np.stack([-sin, cos], -1)], 1)
    up = up.transpose(3, 2, 0, 1).reshape(2 * NA, 2 * MODES)
    down = np.stack([np.stack([cos, sin], 1), np.stack([-sin, cos], 1)], 1)
    turned = np.stack([-down[:, 1], down[:, 0]], 1)
    down = np.concatenate([down.reshape(2 * MODES, 2 * NA), turned.reshape(2 * MODES, 2 * NA)], 0)
    return up.astype(BF), down.astype(BF)


def offsets(bodies):
    ydim = bodies // ZDIM
    far = lambda d, n: min(d, n - d)
    order = [(dy, dz) for dy in range(ydim) for dz in range(ZDIM)]
    order.sort(key=lambda o: (-far(o[0], ydim), -far(o[1], ZDIM), o))
    return order


def target(body, dy, dz, ydim):
    return lax.rem(body // ZDIM + dy, ydim) * ZDIM + lax.rem(lax.rem(body, ZDIM) + dz, ZDIM)


def dot_nt(left, right):
    return lax.dot_general(left, right, (((1,), (1,)), ((), ())), preferred_element_type=F32)


def kernel(
    n_mode, n_body, near_hbm, counts_hbm, nodes_hbm, up_hbm, down_hbm, inc_hbm, w_hbm, inv_hbm, coup_hbm,
    out_ref,
    near_s, near_v, counts_v, nodes_v, up_v, down_v, inc_v, w_v, inv_v, coup_v,
    picks, onehot, dbuf, dens, snd1, recv1a, recv1b, snd3, recv3, rbuf, wall,
    load_sem, send_sem, recv_sem, ready_sem,
):
    me = lax.axis_index("mode")
    body = lax.axis_index("body")
    ydim = n_body // ZDIM
    modes, incs = inv_v.shape[0], inc_v.shape[2]
    near, cap = nodes_v.shape[0], nodes_v.shape[2]
    tiles = rbuf.shape[0]
    order = offsets(n_body)

    pairs = [(inc_hbm, inc_v), (near_hbm, near_v), (counts_hbm, counts_v), (nodes_hbm, nodes_v)]
    pairs += [(inv_hbm.at[k], inv_v.at[k]) for k in range(modes)]
    pairs += [(near_hbm, near_s), (up_hbm, up_v), (down_hbm, down_v), (w_hbm, w_v), (coup_hbm, coup_v)]
    loads = [pltpu.make_async_copy(src, dst, load_sem.at[j]) for j, (src, dst) in enumerate(pairs)]
    load_inc, load_near, load_counts, load_nodes = loads[:4]
    load_inv, (load_near_s, load_up, load_down, load_w, load_coup) = loads[4 : 4 + modes], loads[4 + modes :]

    barrier = pltpu.get_barrier_semaphore()
    for dy, dz in order[:-1]:
        pl.semaphore_signal(
            barrier, inc=1, device_id={"body": target(body, dy, dz, ydim)}, device_id_type=MESH
        )
    for off in range(1, n_mode):
        pl.semaphore_signal(
            barrier, inc=1, device_id={"mode": lax.rem(me + off, n_mode)}, device_id_type=MESH
        )
    for load in loads:
        load.start()

    load_near.wait()
    load_counts.wait()
    load_nodes.wait()
    near_t = jnp.transpose(near_v[...])
    counts_t = jnp.transpose(counts_v[...])
    slot = lax.broadcasted_iota(jnp.int32, (n_body, cap), 1)
    chosen = jnp.full((n_body, cap), -1, jnp.int32)
    for n in range(near):
        ours = jnp.broadcast_to(near_t[:, n : n + 1], (n_body, cap)) == body
        live = slot < jnp.broadcast_to(counts_t[:, n : n + 1], (n_body, cap))
        chosen = jnp.where(ours & live, nodes_v[n], chosen)
    picks[...] = jnp.concatenate([chosen, chosen], 1)

    groups, width = onehot.shape[0], onehot.shape[2]
    per_group = width // cap
    node_index = lax.broadcasted_iota(jnp.int32, (onehot.shape[1], 2 * cap), 0)
    low = lax.broadcasted_iota(jnp.int32, (1, 2 * cap), 1) < cap
    for r in range(0, n_body, 2):
        first, second = (picks[pl.ds(target(body, *order[r + j], ydim), 1), :] for j in range(2))
        row = jnp.where(low, first, second)
        lanes = (r % per_group) * cap
        onehot[r // per_group, :, lanes : lanes + 2 * cap] = jnp.where(node_index == row, 1.0, 0.0).astype(BF)

    def arrived(dst, slot):
        pltpu.make_async_copy(dst, dst, recv_sem.at[slot]).wait()

    def sent(part, slot):
        pltpu.make_async_copy(part, part, send_sem.at[slot]).wait()

    shape = (n_mode, 2 * modes, 2 * cap)
    keep = (lax.broadcasted_iota(jnp.int32, shape, 1) < modes) == (lax.broadcasted_iota(jnp.int32, shape, 2) < cap)

    def swap_quadrants(block):
        return jnp.where(keep, block, pltpu.roll(pltpu.roll(block, modes, 1), cap, 2))

    def inverse_product(k, real, imag):
        first = jnp.concatenate([real, imag], 0).astype(BF)
        second = jnp.concatenate([-imag, real], 0).astype(BF)
        return dot_nt(first, inv_v[k, 0]) + dot_nt(second, inv_v[k, 1])

    def hold(k, value):
        for q in range(tiles):
            dbuf[q, 2 * incs * k : 2 * incs * (k + 1)] = value[:, 128 * q : 128 * q + 128]

    load_inc.wait()
    for k in range(modes):
        load_inv[k].wait()
        hold(k, inverse_product(k, inc_v[k, 0].astype(F32), inc_v[k, 1].astype(F32)))

    for it in range(ITERS):
        to_body, from_body = snd1.at[it], (recv1a, recv1b)[it]

        def send_group(g, it=it, to_body=to_body, from_body=from_body):
            for r in range(g * per_group, (g + 1) * per_group):
                there = target(body, *order[r], ydim)
                last = r == n_body - 1
                for off in range(1 if last else 0, n_mode):
                    peer = lax.rem(me + off, n_mode)
                    pltpu.make_async_remote_copy(
                        src_ref=to_body.at[r, peer], dst_ref=from_body.at[body, me],
                        send_sem=send_sem.at[2 * it], recv_sem=recv_sem.at[2 * it],
                        device_id={"mode": peer, "body": there}, device_id_type=MESH,
                    ).start()
                if last:
                    pltpu.make_async_copy(
                        to_body.at[r, me], from_body.at[body, me], recv_sem.at[2 * it]
                    ).start()

        for i in range(incs):
            rows = [dbuf[q, pl.ds(i, 2 * modes, stride=incs), :] for q in range(tiles)]
            dens[2 * modes * i : 2 * modes * (i + 1)] = jnp.concatenate(rows, 1)
        all_dens = dens[...].astype(BF)

        if it == 0:
            pl.semaphore_wait(barrier, n_body + n_mode - 2)
            for off in range(1, n_mode):
                pl.semaphore_signal(
                    ready_sem, inc=1, device_id={"mode": lax.rem(me + off, n_mode)}, device_id_type=MESH
                )
        for g in range(groups):
            picked = jnp.dot(all_dens, onehot[g], preferred_element_type=F32)
            for pair in range(per_group // 2):
                part = picked[:, 128 * pair : 128 * pair + 128].reshape(shape)
                part = swap_quadrants(part).astype(BF)
                r = g * per_group + 2 * pair
                snd1[it, r] = part[:, :modes]
                snd1[it, r + 1] = part[:, modes:]
            if it == 0 and g == 1:
                pl.semaphore_wait(ready_sem, n_mode - 1)
            if g > 0:
                send_group(g - 1)
        send_group(groups - 1)

        if it == 0:
            load_w.wait()
            for off in range(1, n_mode):
                pltpu.make_async_remote_copy(
                    src_ref=w_v, dst_ref=wall.at[me], send_sem=send_sem.at[4], recv_sem=recv_sem.at[4],
                    device_id={"mode": lax.rem(me + off, n_mode)}, device_id_type=MESH,
                ).start()
            pltpu.make_async_copy(w_v, wall.at[me], recv_sem.at[4]).start()
            load_near_s.wait()
            load_up.wait()
            load_down.wait()
            load_coup.wait()

        arrived(from_body, 2 * it)
        modal = []
        for v in range(0, near, 2):
            both = [from_body[near_s[v + j, body]].astype(F32) for j in range(2)]
            modal.append(swap_quadrants(jnp.concatenate(both, 1)).reshape(2 * MODES, 2 * cap))
        modal = jnp.concatenate(modal, 1).astype(BF)
        cycles = jnp.dot(up_v[...], modal, preferred_element_type=F32)
        if it == 0:
            arrived(wall, 4)
        weights = wall[...].astype(F32).reshape(NA, -1)
        scaled = jnp.concatenate([cycles[:NA] * weights, cycles[NA:] * weights], 0).astype(BF)
        back = jnp.dot(down_v[...], scaled, preferred_element_type=F32).astype(BF)
        half = back.shape[0] // 2
        correction = dot_nt(back[:half], coup_v[0]) + dot_nt(back[half:], coup_v[1])
        for j in range(n_mode):
            snd3[it, j] = correction[2 * modes * j : 2 * modes * (j + 1)].astype(BF)
        for off in range(1, n_mode):
            peer = lax.rem(me + off, n_mode)
            pltpu.make_async_remote_copy(
                src_ref=snd3.at[it, peer], dst_ref=recv3.at[it, me], send_sem=send_sem.at[2 * it + 1],
                recv_sem=recv_sem.at[2 * it + 1], device_id={"mode": peer}, device_id_type=MESH,
            ).start()
        pltpu.make_async_copy(snd3.at[it, me], recv3.at[it, me], recv_sem.at[2 * it + 1]).start()
        arrived(recv3.at[it], 2 * it + 1)

        for i in range(incs):
            value = recv3[it, i].astype(F32)
            for q in range(tiles):
                rbuf[q, 2 * modes * i : 2 * modes * (i + 1)] = value[:, 128 * q : 128 * q + 128]
        for k in range(modes):
            sides = []
            for c in range(2):
                value = [rbuf[q, pl.ds(2 * k + c, incs, stride=2 * modes), :] for q in range(tiles)]
                value = jnp.concatenate(value, 1)
                sides.append(inc_v[k, c].astype(F32) - value * (1.0 / NA))
            value = inverse_product(k, *sides)
            if it < ITERS - 1:
                hold(k, value)
            else:
                out_ref[2 * incs * k : 2 * incs * (k + 1)] = value.astype(BF)

    for it in range(ITERS):
        sent(snd1.at[it, pl.ds(0, n_body - 1)], 2 * it)
        sent(snd1.at[it, n_body - 1, pl.ds(0, n_mode - 1)], 2 * it)
        sent(snd3.at[it, pl.ds(0, n_mode - 1)], 2 * it + 1)
    sent(wall.at[pl.ds(0, n_mode - 1)], 4)


def solution(mesh):
    n_mode, n_body = mesh.shape["mode"], mesh.shape["body"]
    up, down = tables()

    def local(incident, inverse, coupling, cycle_weight, near_bodies, cycle_nodes, cycle_counts):
        bodies, near = near_bodies.shape
        cap = cycle_nodes.shape[2]
        modes, inc, nodes = incident.shape[1], incident.shape[3], incident.shape[4]
        slots = near * cap
        rows = modes * 2 * inc
        width = 4 * cap
        hbm = pl.BlockSpec(memory_space=pl.ANY)
        out = pl.pallas_call(
            lambda *refs: kernel(n_mode, n_body, *refs),
            out_shape=jax.ShapeDtypeStruct((rows, nodes), BF),
            in_specs=[hbm] * 9,
            out_specs=pl.BlockSpec(memory_space=pltpu.VMEM),
            scratch_shapes=[
                pltpu.SMEM((near, bodies), jnp.int32),
                pltpu.VMEM((near, bodies), jnp.int32),
                pltpu.VMEM((near, bodies), jnp.int32),
                pltpu.VMEM((near, bodies, cap), jnp.int32),
                pltpu.VMEM((2 * NA, 2 * MODES), BF),
                pltpu.VMEM((4 * MODES, 2 * NA), BF),
                pltpu.VMEM((modes, 2, inc, nodes), BF),
                pltpu.VMEM((NA // n_mode, slots), BF),
                pltpu.VMEM((modes, 2, nodes, nodes), BF),
                pltpu.VMEM((2, nodes, slots), BF),
                pltpu.VMEM((bodies, 2 * cap), jnp.int32),
                pltpu.VMEM((bodies * cap // width, nodes, width), BF),
                pltpu.VMEM((nodes // 128, rows, 128), F32),
                pltpu.VMEM((rows, nodes), F32),
                pltpu.VMEM((ITERS, bodies, n_mode, modes, 2 * cap), BF),
                pltpu.VMEM((bodies, n_mode, modes, 2 * cap), BF),
                pltpu.VMEM((bodies, n_mode, modes, 2 * cap), BF),
                pltpu.VMEM((ITERS, n_mode, 2 * modes, nodes), BF),
                pltpu.VMEM((ITERS, n_mode, 2 * modes, nodes), BF),
                pltpu.VMEM((nodes // 128, rows, 128), F32),
                pltpu.VMEM((n_mode, NA // n_mode, slots), BF),
                pltpu.SemaphoreType.DMA((modes + 9,)),
                pltpu.SemaphoreType.DMA((2 * ITERS + 1,)),
                pltpu.SemaphoreType.DMA((2 * ITERS + 1,)),
                pltpu.SemaphoreType.REGULAR,
            ],
            compiler_params=pltpu.CompilerParams(collective_id=0, has_side_effects=True),
            name="sweeps",
        )(
            near_bodies.T, cycle_counts.T, cycle_nodes.transpose(1, 0, 2), jnp.asarray(up), jnp.asarray(down),
            incident[0], cycle_weight[0], inverse[0], coupling[0],
        )
        return out.reshape(1, modes, 2, inc, nodes)

    in_specs = (
        P("body", "mode", None, None, None),
        P("body", "mode", None, None, None),
        P("body", None, None, None),
        P("body", "mode", None),
        P(),
        P(),
        P(),
    )
    out_specs = P("body", "mode", None, None, None)
    return jax.shard_map(local, mesh=mesh, in_specs=in_specs, out_specs=out_specs, check_vma=False)
```

```python
import math

import jax
import jax.numpy as jnp
import numpy as np
from jax import lax
from jax.experimental import pallas as pl
from jax.experimental.pallas import tpu as pltpu
from jax.sharding import PartitionSpec as P

MODES = 32
NA = 256
ITERS = 2
ZDIM = 8
MESH = pl.DeviceIdType.MESH
BF = jnp.bfloat16
F32 = jnp.float32


def tables():
    wavenum = np.arange(MODES) - MODES // 2
    residue = (wavenum[:, None] * np.arange(NA)[None, :]) % NA
    theta = residue.astype(np.float32) * np.float32(2.0 * math.pi / NA)
    cos, sin = np.cos(theta), np.sin(theta)
    up = np.stack([np.stack([cos, sin], -1), np.stack([-sin, cos], -1)], 1)
    up = up.transpose(3, 2, 0, 1).reshape(2 * NA, 2 * MODES)
    down = np.stack([np.stack([cos, sin], 1), np.stack([-sin, cos], 1)], 1)
    turned = np.stack([-down[:, 1], down[:, 0]], 1)
    down = np.concatenate([down.reshape(2 * MODES, 2 * NA), turned.reshape(2 * MODES, 2 * NA)], 0)
    return up.astype(BF), down.astype(BF)


def offsets(bodies):
    ydim = bodies // ZDIM
    far = lambda d, n: min(d, n - d)
    order = [(dy, dz) for dy in range(ydim) for dz in range(ZDIM)]
    order.sort(key=lambda o: (-far(o[0], ydim), -far(o[1], ZDIM), o))
    return order


def target(body, dy, dz, ydim):
    return lax.rem(body // ZDIM + dy, ydim) * ZDIM + lax.rem(lax.rem(body, ZDIM) + dz, ZDIM)


def dot_nt(left, right):
    return lax.dot_general(left, right, (((1,), (1,)), ((), ())), preferred_element_type=F32)


def kernel(
    n_mode, n_body, near_hbm, counts_hbm, nodes_hbm, up_hbm, down_hbm, inc_hbm, w_hbm, inv_hbm, coup_hbm,
    out_ref,
    near_s, near_v, counts_v, nodes_v, up_v, down_v, inc_v, w_v, inv_v, coup_v,
    picks, onehot, dbuf, dens, snd1, recv1a, recv1b, snd3, recv3, rbuf, wall,
    load_sem, send_sem, recv_sem, ready_sem,
):
    me = lax.axis_index("mode")
    body = lax.axis_index("body")
    xdim = n_mode // 2
    x, core = me // 2, lax.rem(me, 2)
    mine = core * xdim + x
    ydim = n_body // ZDIM
    modes, incs = inv_v.shape[0], inc_v.shape[2]
    part = incs // 2
    near, cap = nodes_v.shape[0], nodes_v.shape[2]
    tiles = rbuf.shape[1]
    order = offsets(n_body)
    across = sorted(range(xdim), key=lambda dx: -min(dx, xdim - dx))
    peers = sorted(range(1, n_mode), key=lambda off: -min(off, n_mode - off))

    pairs = [(inc_hbm, inc_v), (near_hbm, near_v), (counts_hbm, counts_v), (nodes_hbm, nodes_v)]
    pairs += [(inv_hbm.at[k], inv_v.at[k]) for k in range(modes)]
    pairs += [(near_hbm, near_s), (up_hbm, up_v), (down_hbm, down_v), (w_hbm, w_v), (coup_hbm, coup_v)]
    loads = [pltpu.make_async_copy(src, dst, load_sem.at[j]) for j, (src, dst) in enumerate(pairs)]
    load_inc, load_near, load_counts, load_nodes = loads[:4]
    load_inv, (load_near_s, load_up, load_down, load_w, load_coup) = loads[4 : 4 + modes], loads[4 + modes :]

    barrier = pltpu.get_barrier_semaphore()
    for dy, dz in order[:-1]:
        pl.semaphore_signal(
            barrier, inc=1, device_id={"body": target(body, dy, dz, ydim)}, device_id_type=MESH
        )
    for off in peers:
        pl.semaphore_signal(
            barrier, inc=1, device_id={"mode": lax.rem(me + off, n_mode)}, device_id_type=MESH
        )
    for load in loads:
        load.start()

    load_near.wait()
    load_counts.wait()
    load_nodes.wait()
    near_t = jnp.transpose(near_v[...])
    counts_t = jnp.transpose(counts_v[...])
    slot = lax.broadcasted_iota(jnp.int32, (n_body, cap), 1)
    chosen = jnp.full((n_body, cap), -1, jnp.int32)
    for n in range(near):
        ours = jnp.broadcast_to(near_t[:, n : n + 1], (n_body, cap)) == body
        live = slot < jnp.broadcast_to(counts_t[:, n : n + 1], (n_body, cap))
        chosen = jnp.where(ours & live, nodes_v[n], chosen)
    picks[...] = jnp.concatenate([chosen, chosen], 1)

    groups, width = onehot.shape[0], onehot.shape[2]
    per_group = width // cap
    node_index = lax.broadcasted_iota(jnp.int32, (onehot.shape[1], 2 * cap), 0)
    low = lax.broadcasted_iota(jnp.int32, (1, 2 * cap), 1) < cap
    for r in range(0, n_body, 2):
        first, second = (picks[pl.ds(target(body, *order[r + j], ydim), 1), :] for j in range(2))
        row = jnp.where(low, first, second)
        lanes = (r % per_group) * cap
        onehot[r // per_group, :, lanes : lanes + 2 * cap] = jnp.where(node_index == row, 1.0, 0.0).astype(BF)

    def arrived(dst, slot):
        pltpu.make_async_copy(dst, dst, recv_sem.at[slot]).wait()

    def sent(block, slot):
        pltpu.make_async_copy(block, block, send_sem.at[slot]).wait()

    def swap_quadrants(block):
        up_half = lax.broadcasted_iota(jnp.int32, block.shape, 1) < modes
        left_half = lax.broadcasted_iota(jnp.int32, block.shape, 2) < cap
        return jnp.where(up_half == left_half, block, pltpu.roll(pltpu.roll(block, modes, 1), cap, 2))

    def inverse_product(k, sides):
        first = jnp.concatenate([v for real, imag in sides for v in (real, imag)], 0).astype(BF)
        second = jnp.concatenate([v for real, imag in sides for v in (-imag, real)], 0).astype(BF)
        return dot_nt(first, inv_v[k, 0]) + dot_nt(second, inv_v[k, 1])

    def hold(k, h, value):
        for q in range(tiles):
            dbuf[h, q, 2 * part * k : 2 * part * (k + 1)] = value[:, 128 * q : 128 * q + 128]

    def density_rows(h):
        for i in range(part):
            rows = [dbuf[h, q, pl.ds(i, 2 * modes, stride=part), :] for q in range(tiles)]
            dens[h, 2 * modes * i : 2 * modes * (i + 1)] = jnp.concatenate(rows, 1)
        return dens[h].astype(BF)

    def gather(it, h, g, rows):
        picked = jnp.dot(rows, onehot[g], preferred_element_type=F32)
        for pair in range(per_group // 2):
            block = picked[:, 128 * pair : 128 * pair + 128].reshape(part, 2 * modes, 2 * cap)
            block = swap_quadrants(block).astype(BF)
            r = g * per_group + 2 * pair
            snd1[it, r, part * h : part * (h + 1)] = block[:, :modes]
            snd1[it, r + 1, part * h : part * (h + 1)] = block[:, modes:]

    def post(it, r, to_x, to_core):
        pltpu.make_async_remote_copy(
            src_ref=snd1.at[it, r, to_core * xdim + to_x], dst_ref=(recv1a, recv1b)[it].at[body, me],
            send_sem=send_sem.at[2 * it], recv_sem=recv_sem.at[it],
            device_id={"mode": 2 * to_x + to_core, "body": target(body, *order[r], ydim)},
            device_id_type=MESH,
        ).start()

    def keep_own(it):
        pltpu.make_async_copy(
            snd1.at[it, n_body - 1, mine], (recv1a, recv1b)[it].at[body, me], recv_sem.at[it]
        ).start()

    load_inc.wait()
    for k in range(modes):
        load_inv[k].wait()
        real, imag = inc_v[k, 0].astype(F32), inc_v[k, 1].astype(F32)
        cut = [slice(part * h, part * (h + 1)) for h in range(2)]
        value = inverse_product(k, [(real[c], imag[c]) for c in cut])
        for h in range(2):
            hold(k, h, value[2 * part * h : 2 * part * (h + 1)])
    for h in range(2):
        rows = density_rows(h)
        for g in range(groups):
            gather(0, h, g, rows)

    pl.semaphore_wait(barrier, n_body + n_mode - 2)
    for off in peers:
        pl.semaphore_signal(
            ready_sem, inc=1, device_id={"mode": lax.rem(me + off, n_mode)}, device_id_type=MESH
        )
    for r in range(n_body - 1):
        post(0, r, x, core)
    pl.semaphore_wait(ready_sem, n_mode - 1)
    for h in range(2):
        for r in range(n_body):
            for dx in across[:-1]:
                post(0, r, lax.rem(x + dx, xdim), h)
        if h == 0:
            for r in range(n_body):
                post(0, r, x, 1 - core)
    keep_own(0)

    load_w.wait()
    for off in peers:
        pltpu.make_async_remote_copy(
            src_ref=w_v, dst_ref=wall.at[me], send_sem=send_sem.at[4], recv_sem=recv_sem.at[6],
            device_id={"mode": lax.rem(me + off, n_mode)}, device_id_type=MESH,
        ).start()
    pltpu.make_async_copy(w_v, wall.at[me], recv_sem.at[6]).start()
    load_near_s.wait()
    load_up.wait()
    load_down.wait()
    load_coup.wait()

    for it in range(ITERS):
        from_body = (recv1a, recv1b)[it]
        arrived(from_body, it)
        modal = []
        for v in range(0, near, 2):
            both = [from_body[near_s[v + j, body]].astype(F32) for j in range(2)]
            modal.append(swap_quadrants(jnp.concatenate(both, 1)).reshape(2 * MODES, 2 * cap))
        modal = jnp.concatenate(modal, 1).astype(BF)
        cycles = jnp.dot(up_v[...], modal, preferred_element_type=F32)
        if it == 0:
            arrived(wall, 6)
        weights = wall[...].astype(F32).reshape(NA, -1)
        scaled = jnp.concatenate([cycles[:NA] * weights, cycles[NA:] * weights], 0).astype(BF)
        back = jnp.dot(down_v[...], scaled, preferred_element_type=F32).astype(BF)
        half = back.shape[0] // 2
        correction = dot_nt(back[:half], coup_v[0]) + dot_nt(back[half:], coup_v[1])
        for j in range(n_mode):
            snd3[it, j] = correction[2 * modes * j : 2 * modes * (j + 1)].astype(BF)
        for off in peers:
            peer = lax.rem(me + off, n_mode)
            pltpu.make_async_remote_copy(
                src_ref=snd3.at[it, peer], dst_ref=recv3.at[it, mine], send_sem=send_sem.at[2 * it + 1],
                recv_sem=recv_sem.at[2 + 2 * it + core], device_id={"mode": peer}, device_id_type=MESH,
            ).start()
        pltpu.make_async_copy(snd3.at[it, me], recv3.at[it, mine], recv_sem.at[2 + 2 * it + core]).start()

        for h in range(2):
            arrived(recv3.at[it, pl.ds(part * h, part)], 2 + 2 * it + h)
            for i in range(part):
                value = recv3[it, part * h + i].astype(F32)
                for q in range(tiles):
                    rbuf[h, q, 2 * modes * i : 2 * modes * (i + 1)] = value[:, 128 * q : 128 * q + 128]
            for k in range(modes):
                sides = []
                for c in range(2):
                    value = [rbuf[h, q, pl.ds(2 * k + c, part, stride=2 * modes), :] for q in range(tiles)]
                    value = jnp.concatenate(value, 1)
                    source = inc_v[k, c].astype(F32)[part * h : part * (h + 1)]
                    sides.append(source - value * (1.0 / NA))
                value = inverse_product(k, [sides])
                if it == ITERS - 1 and h == 1:
                    early = [dbuf[0, q, 2 * part * k : 2 * part * (k + 1)] for q in range(tiles)]
                    early = jnp.concatenate(early, 1)
                    value = [early[:part], value[:part], early[part:], value[part:]]
                    value = jnp.concatenate(value, 0)
                    out_ref[2 * incs * k : 2 * incs * (k + 1)] = value.astype(BF)
                else:
                    hold(k, h, value)
            if it < ITERS - 1:
                rows = density_rows(h)
                for g in range(groups + 1):
                    if g < groups:
                        gather(it + 1, h, g, rows)
                    if g > 0:
                        for r in range((g - 1) * per_group, g * per_group):
                            for dx in across if r < n_body - 1 else across[:-1]:
                                post(it + 1, r, lax.rem(x + dx, xdim), h)
                if h == 1:
                    post(it + 1, n_body - 1, x, 1 - core)
                    keep_own(it + 1)

    for it in range(ITERS):
        sent(snd1.at[it, pl.ds(0, n_body - 1)], 2 * it)
        sent(snd1.at[it, n_body - 1, pl.ds(0, n_mode - 1)], 2 * it)
        sent(snd3.at[it, pl.ds(0, n_mode - 1)], 2 * it + 1)
    sent(wall.at[pl.ds(0, n_mode - 1)], 4)


def solution(mesh):
    n_mode, n_body = mesh.shape["mode"], mesh.shape["body"]
    up, down = tables()

    def local(incident, inverse, coupling, cycle_weight, near_bodies, cycle_nodes, cycle_counts):
        bodies, near = near_bodies.shape
        cap = cycle_nodes.shape[2]
        modes, inc, nodes = incident.shape[1], incident.shape[3], incident.shape[4]
        slots = near * cap
        rows = modes * 2 * inc
        width = 4 * cap
        hbm = pl.BlockSpec(memory_space=pl.ANY)
        out = pl.pallas_call(
            lambda *refs: kernel(n_mode, n_body, *refs),
            out_shape=pltpu.VMEM((rows, nodes), BF),
            in_specs=[hbm] * 9,
            out_specs=pl.BlockSpec(memory_space=pltpu.VMEM),
            scratch_shapes=[
                pltpu.SMEM((near, bodies), jnp.int32),
                pltpu.VMEM((near, bodies), jnp.int32),
                pltpu.VMEM((near, bodies), jnp.int32),
                pltpu.VMEM((near, bodies, cap), jnp.int32),
                pltpu.VMEM((2 * NA, 2 * MODES), BF),
                pltpu.VMEM((4 * MODES, 2 * NA), BF),
                pltpu.VMEM((modes, 2, inc, nodes), BF),
                pltpu.VMEM((NA // n_mode, slots), BF),
                pltpu.VMEM((modes, 2, nodes, nodes), BF),
                pltpu.VMEM((2, nodes, slots), BF),
                pltpu.VMEM((bodies, 2 * cap), jnp.int32),
                pltpu.VMEM((bodies * cap // width, nodes, width), BF),
                pltpu.VMEM((2, nodes // 128, rows // 2, 128), F32),
                pltpu.VMEM((2, rows // 2, nodes), F32),
                pltpu.VMEM((ITERS, bodies, n_mode, modes, 2 * cap), BF),
                pltpu.VMEM((bodies, n_mode, modes, 2 * cap), BF),
                pltpu.VMEM((bodies, n_mode, modes, 2 * cap), BF),
                pltpu.VMEM((ITERS, n_mode, 2 * modes, nodes), BF),
                pltpu.VMEM((ITERS, n_mode, 2 * modes, nodes), BF),
                pltpu.VMEM((2, nodes // 128, rows // 2, 128), F32),
                pltpu.VMEM((n_mode, NA // n_mode, slots), BF),
                pltpu.SemaphoreType.DMA((modes + 9,)),
                pltpu.SemaphoreType.DMA((2 * ITERS + 1,)),
                pltpu.SemaphoreType.DMA((3 * ITERS + 1,)),
                pltpu.SemaphoreType.REGULAR,
            ],
            compiler_params=pltpu.CompilerParams(collective_id=0, has_side_effects=True),
            name="sweeps",
        )(
            near_bodies.T, cycle_counts.T, cycle_nodes.transpose(1, 0, 2), jnp.asarray(up), jnp.asarray(down),
            incident[0], cycle_weight[0], inverse[0], coupling[0],
        )
        return out.reshape(1, modes, 2, inc, nodes)

    in_specs = (
        P("body", "mode", None, None, None),
        P("body", "mode", None, None, None),
        P("body", None, None, None),
        P("body", "mode", None),
        P(),
        P(),
        P(),
    )
    out_specs = P("body", "mode", None, None, None)
    return jax.shard_map(local, mesh=mesh, in_specs=in_specs, out_specs=out_specs, check_vma=False)
```

```python
import math

import jax
import jax.numpy as jnp
import numpy as np
from jax import lax
from jax.experimental import pallas as pl
from jax.experimental.pallas import tpu as pltpu
from jax.sharding import PartitionSpec as P

MODES = 32
NA = 256
ITERS = 2
ZDIM = 8
MESH = pl.DeviceIdType.MESH
BF = jnp.bfloat16
F32 = jnp.float32


def tables():
    wavenum = np.arange(MODES) - MODES // 2
    residue = (wavenum[:, None] * np.arange(NA)[None, :]) % NA
    theta = residue.astype(np.float32) * np.float32(2.0 * math.pi / NA)
    cos, sin = np.cos(theta), np.sin(theta)
    up = np.stack([np.stack([cos, sin], -1), np.stack([-sin, cos], -1)], 1)
    up = up.transpose(3, 2, 0, 1).reshape(2 * NA, 2 * MODES)
    down = np.stack([np.stack([cos, sin], 1), np.stack([-sin, cos], 1)], 1)
    turned = np.stack([-down[:, 1], down[:, 0]], 1)
    down = np.concatenate([down.reshape(2 * MODES, 2 * NA), turned.reshape(2 * MODES, 2 * NA)], 0)
    return up.astype(BF), down.astype(BF)


def offsets(bodies):
    ydim = bodies // ZDIM
    far = lambda d, n: min(d, n - d)
    order = [(dy, dz) for dy in range(ydim) for dz in range(ZDIM)]
    order.sort(key=lambda o: (-far(o[0], ydim), -far(o[1], ZDIM), o))
    return order


def target(body, dy, dz, ydim):
    return lax.rem(body // ZDIM + dy, ydim) * ZDIM + lax.rem(lax.rem(body, ZDIM) + dz, ZDIM)


def dot_nt(left, right):
    return lax.dot_general(left, right, (((1,), (1,)), ((), ())), preferred_element_type=F32)


def kernel(
    n_mode, n_body, near_hbm, counts_hbm, nodes_hbm, up_hbm, down_hbm, inc_hbm, w_hbm, inv_hbm, coup_hbm,
    out_ref,
    near_s, near_v, counts_v, nodes_v, up_v, down_v, inc_v, w_v, inv_v, coup_v, inv_t, coup_t,
    picks, onehot, dbuf, dens, snd1, recv1a, recv1b, snd3, recv3, rbuf, wall,
    load_sem, send_sem, recv_sem, ready_sem,
):
    me = lax.axis_index("mode")
    body = lax.axis_index("body")
    xdim = n_mode // 2
    x, core = me // 2, lax.rem(me, 2)
    mine = core * xdim + x
    ydim = n_body // ZDIM
    modes, incs = inv_v.shape[0], inc_v.shape[2]
    part = incs // 2
    near, cap = nodes_v.shape[0], nodes_v.shape[2]
    tiles = rbuf.shape[1]
    order = offsets(n_body)
    across = sorted(range(xdim), key=lambda dx: -min(dx, xdim - dx))
    peers = sorted(range(1, n_mode), key=lambda off: -min(off, n_mode - off))

    pairs = [(inc_hbm, inc_v), (near_hbm, near_v), (counts_hbm, counts_v), (nodes_hbm, nodes_v)]
    pairs += [(inv_hbm.at[k], inv_v.at[k]) for k in range(modes)]
    pairs += [(near_hbm, near_s), (up_hbm, up_v), (down_hbm, down_v), (w_hbm, w_v), (coup_hbm, coup_v)]
    loads = [pltpu.make_async_copy(src, dst, load_sem.at[j]) for j, (src, dst) in enumerate(pairs)]
    load_inc, load_near, load_counts, load_nodes = loads[:4]
    load_inv, (load_near_s, load_up, load_down, load_w, load_coup) = loads[4 : 4 + modes], loads[4 + modes :]

    barrier = pltpu.get_barrier_semaphore()
    for dy, dz in order[:-1]:
        pl.semaphore_signal(
            barrier, inc=1, device_id={"body": target(body, dy, dz, ydim)}, device_id_type=MESH
        )
    for off in peers:
        pl.semaphore_signal(
            barrier, inc=1, device_id={"mode": lax.rem(me + off, n_mode)}, device_id_type=MESH
        )
    for load in loads:
        load.start()

    load_near.wait()
    load_counts.wait()
    load_nodes.wait()
    near_t = jnp.transpose(near_v[...])
    counts_t = jnp.transpose(counts_v[...])
    slot = lax.broadcasted_iota(jnp.int32, (n_body, cap), 1)
    chosen = jnp.full((n_body, cap), -1, jnp.int32)
    for n in range(near):
        ours = jnp.broadcast_to(near_t[:, n : n + 1], (n_body, cap)) == body
        live = slot < jnp.broadcast_to(counts_t[:, n : n + 1], (n_body, cap))
        chosen = jnp.where(ours & live, nodes_v[n], chosen)
    picks[...] = jnp.concatenate([chosen, chosen], 1)

    groups, width = onehot.shape[0], onehot.shape[2]
    per_group = width // cap
    node_index = lax.broadcasted_iota(jnp.int32, (onehot.shape[1], 2 * cap), 0)
    low = lax.broadcasted_iota(jnp.int32, (1, 2 * cap), 1) < cap
    for r in range(0, n_body, 2):
        first, second = (picks[pl.ds(target(body, *order[r + j], ydim), 1), :] for j in range(2))
        row = jnp.where(low, first, second)
        lanes = (r % per_group) * cap
        onehot[r // per_group, :, lanes : lanes + 2 * cap] = jnp.where(node_index == row, 1.0, 0.0).astype(BF)

    def arrived(dst, slot):
        pltpu.make_async_copy(dst, dst, recv_sem.at[slot]).wait()

    def sent(block, slot):
        pltpu.make_async_copy(block, block, send_sem.at[slot]).wait()

    def swap_quadrants(block):
        up_half = lax.broadcasted_iota(jnp.int32, block.shape, 1) < modes
        left_half = lax.broadcasted_iota(jnp.int32, block.shape, 2) < cap
        return jnp.where(up_half == left_half, block, pltpu.roll(pltpu.roll(block, modes, 1), cap, 2))

    def inverse_product(k, sides, turned=True):
        first = jnp.concatenate([v for real, imag in sides for v in (real, imag)], 0).astype(BF)
        second = jnp.concatenate([v for real, imag in sides for v in (-imag, real)], 0).astype(BF)
        if turned:
            real = jnp.dot(first, inv_t[k, 0], preferred_element_type=F32)
            return real + jnp.dot(second, inv_t[k, 1], preferred_element_type=F32)
        return dot_nt(first, inv_v[k, 0]) + dot_nt(second, inv_v[k, 1])

    def hold(k, h, value):
        for q in range(tiles):
            dbuf[h, q, 2 * part * k : 2 * part * (k + 1)] = value[:, 128 * q : 128 * q + 128]

    def density_rows(h):
        for i in range(part):
            rows = [dbuf[h, q, pl.ds(i, 2 * modes, stride=part), :] for q in range(tiles)]
            dens[h, 2 * modes * i : 2 * modes * (i + 1)] = jnp.concatenate(rows, 1)
        return dens[h].astype(BF)

    def gather(it, h, g, rows):
        picked = jnp.dot(rows, onehot[g], preferred_element_type=F32)
        for pair in range(per_group // 2):
            block = picked[:, 128 * pair : 128 * pair + 128].reshape(part, 2 * modes, 2 * cap)
            block = swap_quadrants(block).astype(BF)
            r = g * per_group + 2 * pair
            snd1[it, r, part * h : part * (h + 1)] = block[:, :modes]
            snd1[it, r + 1, part * h : part * (h + 1)] = block[:, modes:]

    def post(it, r, to_x, to_core):
        pltpu.make_async_remote_copy(
            src_ref=snd1.at[it, r, to_core * xdim + to_x], dst_ref=(recv1a, recv1b)[it].at[body, me],
            send_sem=send_sem.at[2 * it], recv_sem=recv_sem.at[it],
            device_id={"mode": 2 * to_x + to_core, "body": target(body, *order[r], ydim)},
            device_id_type=MESH,
        ).start()

    def keep_own(it):
        pltpu.make_async_copy(
            snd1.at[it, n_body - 1, mine], (recv1a, recv1b)[it].at[body, me], recv_sem.at[it]
        ).start()

    load_inc.wait()
    for k in range(modes):
        load_inv[k].wait()
        real, imag = inc_v[k, 0].astype(F32), inc_v[k, 1].astype(F32)
        cut = [slice(part * h, part * (h + 1)) for h in range(2)]
        value = inverse_product(k, [(real[c], imag[c]) for c in cut], turned=False)
        for h in range(2):
            hold(k, h, value[2 * part * h : 2 * part * (h + 1)])
    for h in range(2):
        rows = density_rows(h)
        for g in range(groups):
            gather(0, h, g, rows)

    pl.semaphore_wait(barrier, n_body + n_mode - 2)
    for off in peers:
        pl.semaphore_signal(
            ready_sem, inc=1, device_id={"mode": lax.rem(me + off, n_mode)}, device_id_type=MESH
        )
    for r in range(n_body - 1):
        post(0, r, x, core)
    pl.semaphore_wait(ready_sem, n_mode - 1)
    for h in range(2):
        for r in range(n_body):
            for dx in across[:-1]:
                post(0, r, lax.rem(x + dx, xdim), h)
        if h == 0:
            for r in range(n_body):
                post(0, r, x, 1 - core)
    keep_own(0)

    load_w.wait()
    for off in peers:
        pltpu.make_async_remote_copy(
            src_ref=w_v, dst_ref=wall.at[me], send_sem=send_sem.at[4], recv_sem=recv_sem.at[6],
            device_id={"mode": lax.rem(me + off, n_mode)}, device_id_type=MESH,
        ).start()
    pltpu.make_async_copy(w_v, wall.at[me], recv_sem.at[6]).start()
    load_near_s.wait()
    load_up.wait()
    load_down.wait()
    load_coup.wait()

    for c in range(2):
        coup_t[c] = jnp.transpose(coup_v[c])

    @pl.loop(0, modes)
    def _(k):
        for c in range(2):
            inv_t[k, c] = jnp.transpose(inv_v[k, c])

    for it in range(ITERS):
        from_body = (recv1a, recv1b)[it]
        arrived(from_body, it)
        modal = []
        for v in range(0, near, 2):
            both = [from_body[near_s[v + j, body]].astype(F32) for j in range(2)]
            modal.append(swap_quadrants(jnp.concatenate(both, 1)).reshape(2 * MODES, 2 * cap))
        modal = jnp.concatenate(modal, 1).astype(BF)
        cycles = jnp.dot(up_v[...], modal, preferred_element_type=F32)
        if it == 0:
            arrived(wall, 6)
        weights = wall[...].astype(F32).reshape(NA, -1)
        scaled = jnp.concatenate([cycles[:NA] * weights, cycles[NA:] * weights], 0).astype(BF)
        back = jnp.dot(down_v[...], scaled, preferred_element_type=F32).astype(BF)
        half = back.shape[0] // 2
        correction = jnp.dot(back[:half], coup_t[0], preferred_element_type=F32)
        correction = correction + jnp.dot(back[half:], coup_t[1], preferred_element_type=F32)
        for j in range(n_mode):
            snd3[it, j] = correction[2 * modes * j : 2 * modes * (j + 1)].astype(BF)
        for off in peers:
            peer = lax.rem(me + off, n_mode)
            pltpu.make_async_remote_copy(
                src_ref=snd3.at[it, peer], dst_ref=recv3.at[it, mine], send_sem=send_sem.at[2 * it + 1],
                recv_sem=recv_sem.at[2 + 2 * it + core], device_id={"mode": peer}, device_id_type=MESH,
            ).start()
        pltpu.make_async_copy(snd3.at[it, me], recv3.at[it, mine], recv_sem.at[2 + 2 * it + core]).start()

        for h in range(2):
            arrived(recv3.at[it, pl.ds(part * h, part)], 2 + 2 * it + h)
            for i in range(part):
                value = recv3[it, part * h + i].astype(F32)
                for q in range(tiles):
                    rbuf[h, q, 2 * modes * i : 2 * modes * (i + 1)] = value[:, 128 * q : 128 * q + 128]
            for k in range(modes):
                sides = []
                for c in range(2):
                    value = [rbuf[h, q, pl.ds(2 * k + c, part, stride=2 * modes), :] for q in range(tiles)]
                    value = jnp.concatenate(value, 1)
                    source = inc_v[k, c].astype(F32)[part * h : part * (h + 1)]
                    sides.append(source - value * (1.0 / NA))
                value = inverse_product(k, [sides])
                if it == ITERS - 1 and h == 1:
                    early = [dbuf[0, q, 2 * part * k : 2 * part * (k + 1)] for q in range(tiles)]
                    early = jnp.concatenate(early, 1)
                    value = [early[:part], value[:part], early[part:], value[part:]]
                    value = jnp.concatenate(value, 0)
                    out_ref[2 * incs * k : 2 * incs * (k + 1)] = value.astype(BF)
                else:
                    hold(k, h, value)
            if it < ITERS - 1:
                rows = density_rows(h)
                for g in range(groups + 1):
                    if g < groups:
                        gather(it + 1, h, g, rows)
                    if g > 0:
                        for r in range((g - 1) * per_group, g * per_group):
                            for dx in across if r < n_body - 1 else across[:-1]:
                                post(it + 1, r, lax.rem(x + dx, xdim), h)
                if h == 1:
                    post(it + 1, n_body - 1, x, 1 - core)
                    keep_own(it + 1)

    for it in range(ITERS):
        sent(snd1.at[it, pl.ds(0, n_body - 1)], 2 * it)
        sent(snd1.at[it, n_body - 1, pl.ds(0, n_mode - 1)], 2 * it)
        sent(snd3.at[it, pl.ds(0, n_mode - 1)], 2 * it + 1)
    sent(wall.at[pl.ds(0, n_mode - 1)], 4)


def solution(mesh):
    n_mode, n_body = mesh.shape["mode"], mesh.shape["body"]
    up, down = tables()

    def local(incident, inverse, coupling, cycle_weight, near_bodies, cycle_nodes, cycle_counts):
        bodies, near = near_bodies.shape
        cap = cycle_nodes.shape[2]
        modes, inc, nodes = incident.shape[1], incident.shape[3], incident.shape[4]
        slots = near * cap
        rows = modes * 2 * inc
        width = 4 * cap
        hbm = pl.BlockSpec(memory_space=pl.ANY)
        out = pl.pallas_call(
            lambda *refs: kernel(n_mode, n_body, *refs),
            out_shape=pltpu.VMEM((rows, nodes), BF),
            in_specs=[hbm] * 9,
            out_specs=pl.BlockSpec(memory_space=pltpu.VMEM),
            scratch_shapes=[
                pltpu.SMEM((near, bodies), jnp.int32),
                pltpu.VMEM((near, bodies), jnp.int32),
                pltpu.VMEM((near, bodies), jnp.int32),
                pltpu.VMEM((near, bodies, cap), jnp.int32),
                pltpu.VMEM((2 * NA, 2 * MODES), BF),
                pltpu.VMEM((4 * MODES, 2 * NA), BF),
                pltpu.VMEM((modes, 2, inc, nodes), BF),
                pltpu.VMEM((NA // n_mode, slots), BF),
                pltpu.VMEM((modes, 2, nodes, nodes), BF),
                pltpu.VMEM((2, nodes, slots), BF),
                pltpu.VMEM((modes, 2, nodes, nodes), BF),
                pltpu.VMEM((2, slots, nodes), BF),
                pltpu.VMEM((bodies, 2 * cap), jnp.int32),
                pltpu.VMEM((bodies * cap // width, nodes, width), BF),
                pltpu.VMEM((2, nodes // 128, rows // 2, 128), F32),
                pltpu.VMEM((2, rows // 2, nodes), F32),
                pltpu.VMEM((ITERS, bodies, n_mode, modes, 2 * cap), BF),
                pltpu.VMEM((bodies, n_mode, modes, 2 * cap), BF),
                pltpu.VMEM((bodies, n_mode, modes, 2 * cap), BF),
                pltpu.VMEM((ITERS, n_mode, 2 * modes, nodes), BF),
                pltpu.VMEM((ITERS, n_mode, 2 * modes, nodes), BF),
                pltpu.VMEM((2, nodes // 128, rows // 2, 128), F32),
                pltpu.VMEM((n_mode, NA // n_mode, slots), BF),
                pltpu.SemaphoreType.DMA((modes + 9,)),
                pltpu.SemaphoreType.DMA((2 * ITERS + 1,)),
                pltpu.SemaphoreType.DMA((3 * ITERS + 1,)),
                pltpu.SemaphoreType.REGULAR,
            ],
            compiler_params=pltpu.CompilerParams(collective_id=0, has_side_effects=True),
            name="sweeps",
        )(
            near_bodies.T, cycle_counts.T, cycle_nodes.transpose(1, 0, 2), jnp.asarray(up), jnp.asarray(down),
            incident[0], cycle_weight[0], inverse[0], coupling[0],
        )
        return out.reshape(1, modes, 2, inc, nodes)

    in_specs = (
        P("body", "mode", None, None, None),
        P("body", "mode", None, None, None),
        P("body", None, None, None),
        P("body", "mode", None),
        P(),
        P(),
        P(),
    )
    out_specs = P("body", "mode", None, None, None)
    return jax.shard_map(local, mesh=mesh, in_specs=in_specs, out_specs=out_specs, check_vma=False)
```

```python
import math

import jax
import jax.numpy as jnp
import numpy as np
from jax import lax
from jax.experimental import pallas as pl
from jax.experimental.pallas import tpu as pltpu
from jax.sharding import PartitionSpec as P

MODES = 32
NA = 256
ITERS = 2
ZDIM = 8
MESH = pl.DeviceIdType.MESH
BF = jnp.bfloat16
F32 = jnp.float32


def tables():
    wavenum = np.arange(MODES) - MODES // 2
    residue = (wavenum[:, None] * np.arange(NA)[None, :]) % NA
    theta = residue.astype(np.float32) * np.float32(2.0 * math.pi / NA)
    cos, sin = np.cos(theta), np.sin(theta)
    up = np.stack([np.stack([cos, sin], -1), np.stack([-sin, cos], -1)], 1)
    up = up.transpose(3, 2, 0, 1).reshape(2 * NA, 2 * MODES)
    down = np.stack([np.stack([cos, sin], 1), np.stack([-sin, cos], 1)], 1)
    turned = np.stack([-down[:, 1], down[:, 0]], 1)
    down = np.concatenate([down.reshape(2 * MODES, 2 * NA), turned.reshape(2 * MODES, 2 * NA)], 0)
    return up.astype(BF), down.astype(BF)


def offsets(bodies):
    ydim = bodies // ZDIM
    far = lambda d, n: min(d, n - d)
    order = [(dy, dz) for dy in range(ydim) for dz in range(ZDIM)]
    order.sort(key=lambda o: (-far(o[0], ydim), -far(o[1], ZDIM), o))
    return order


def target(body, dy, dz, ydim):
    return lax.rem(body // ZDIM + dy, ydim) * ZDIM + lax.rem(lax.rem(body, ZDIM) + dz, ZDIM)


def dot_nt(left, right):
    return lax.dot_general(left, right, (((1,), (1,)), ((), ())), preferred_element_type=F32)


def kernel(
    n_mode, n_body, near_hbm, counts_hbm, nodes_hbm, up_hbm, down_hbm, inc_hbm, w_hbm, inv_hbm, coup_hbm,
    out_ref,
    near_s, near_v, counts_v, nodes_v, up_v, down_v, inc_v, w_v, inv_v, coup_v, inv_t, coup_t,
    picks, onehot, dbuf, dens, snd1, recv1a, recv1b, snd3, recv3, rbuf, wall,
    load_sem, send_sem, recv_sem, ready_sem,
):
    me = lax.axis_index("mode")
    body = lax.axis_index("body")
    xdim = n_mode // 2
    x, core = me // 2, lax.rem(me, 2)
    mine = core * xdim + x
    ydim = n_body // ZDIM
    modes, incs = inv_v.shape[0], inc_v.shape[2]
    part = incs // 2
    near, cap = nodes_v.shape[0], nodes_v.shape[2]
    tiles = rbuf.shape[1]
    order = offsets(n_body)
    across = sorted(range(xdim), key=lambda dx: -min(dx, xdim - dx))
    peers = sorted(range(1, n_mode), key=lambda off: -min(off, n_mode - off))

    pairs = [(inc_hbm, inc_v), (near_hbm, near_v), (counts_hbm, counts_v), (nodes_hbm, nodes_v)]
    pairs += [(inv_hbm.at[k], inv_v.at[k]) for k in range(modes)]
    pairs += [(near_hbm, near_s), (up_hbm, up_v), (down_hbm, down_v), (w_hbm, w_v), (coup_hbm, coup_v)]
    loads = [pltpu.make_async_copy(src, dst, load_sem.at[j]) for j, (src, dst) in enumerate(pairs)]
    load_inc, load_near, load_counts, load_nodes = loads[:4]
    load_inv, (load_near_s, load_up, load_down, load_w, load_coup) = loads[4 : 4 + modes], loads[4 + modes :]

    for load in loads:
        load.start()

    barrier = pltpu.get_barrier_semaphore()
    for dy, dz in order[:-1]:
        pl.semaphore_signal(
            barrier, inc=1, device_id={"body": target(body, dy, dz, ydim)}, device_id_type=MESH
        )
    for off in peers:
        pl.semaphore_signal(
            barrier, inc=1, device_id={"mode": lax.rem(me + off, n_mode)}, device_id_type=MESH
        )

    load_near.wait()
    load_counts.wait()
    load_nodes.wait()
    near_t = jnp.transpose(near_v[...])
    counts_t = jnp.transpose(counts_v[...])
    slot = lax.broadcasted_iota(jnp.int32, (n_body, cap), 1)
    chosen = jnp.full((n_body, cap), -1, jnp.int32)
    for n in range(near):
        ours = jnp.broadcast_to(near_t[:, n : n + 1], (n_body, cap)) == body
        live = slot < jnp.broadcast_to(counts_t[:, n : n + 1], (n_body, cap))
        chosen = jnp.where(ours & live, nodes_v[n], chosen)
    picks[...] = jnp.concatenate([chosen, chosen], 1)

    groups, width = onehot.shape[0], onehot.shape[2]
    per_group = width // cap
    node_index = lax.broadcasted_iota(jnp.int32, (onehot.shape[1], 2 * cap), 0)
    low = lax.broadcasted_iota(jnp.int32, (1, 2 * cap), 1) < cap
    def build(start, stop):
        for r in range(start, stop, 2):
            first, second = (picks[pl.ds(target(body, *order[r + j], ydim), 1), :] for j in range(2))
            row = jnp.where(low, first, second)
            lanes = (r % per_group) * cap
            hit = jnp.where(node_index == row, 1.0, 0.0).astype(BF)
            onehot[r // per_group, :, lanes : lanes + 2 * cap] = hit

    build(0, n_body // 2)

    def arrived(dst, slot):
        pltpu.make_async_copy(dst, dst, recv_sem.at[slot]).wait()

    def sent(block, slot):
        pltpu.make_async_copy(block, block, send_sem.at[slot]).wait()

    def swap_quadrants(block):
        up_half = lax.broadcasted_iota(jnp.int32, block.shape, 1) < modes
        left_half = lax.broadcasted_iota(jnp.int32, block.shape, 2) < cap
        return jnp.where(up_half == left_half, block, pltpu.roll(pltpu.roll(block, modes, 1), cap, 2))

    def inverse_product(k, sides, turned=True):
        first = jnp.concatenate([v for real, imag in sides for v in (real, imag)], 0).astype(BF)
        second = jnp.concatenate([v for real, imag in sides for v in (-imag, real)], 0).astype(BF)
        if turned:
            right = inv_t[k].reshape(2 * inv_t.shape[2], -1)
            return jnp.dot(jnp.concatenate([first, second], 1), right, preferred_element_type=F32)
        return dot_nt(first, inv_v[k, 0]) + dot_nt(second, inv_v[k, 1])

    def hold(k, h, value):
        for q in range(tiles):
            dbuf[h, q, 2 * part * k : 2 * part * (k + 1)] = value[:, 128 * q : 128 * q + 128]

    def density_rows(h):
        for i in range(part):
            rows = [dbuf[h, q, pl.ds(i, 2 * modes, stride=part), :] for q in range(tiles)]
            dens[h, 2 * modes * i : 2 * modes * (i + 1)] = jnp.concatenate(rows, 1)
        return dens[h].astype(BF)

    def gather(it, h, g, rows):
        picked = jnp.dot(rows, onehot[g], preferred_element_type=F32)
        for pair in range(per_group // 2):
            block = picked[:, 128 * pair : 128 * pair + 128].reshape(part, 2 * modes, 2 * cap)
            block = swap_quadrants(block).astype(BF)
            r = g * per_group + 2 * pair
            snd1[it, r, part * h : part * (h + 1)] = block[:, :modes]
            snd1[it, r + 1, part * h : part * (h + 1)] = block[:, modes:]

    def post(it, r, to_x, to_core):
        pltpu.make_async_remote_copy(
            src_ref=snd1.at[it, r, to_core * xdim + to_x], dst_ref=(recv1a, recv1b)[it].at[body, me],
            send_sem=send_sem.at[2 * it], recv_sem=recv_sem.at[it],
            device_id={"mode": 2 * to_x + to_core, "body": target(body, *order[r], ydim)},
            device_id_type=MESH,
        ).start()

    def keep_own(it):
        pltpu.make_async_copy(
            snd1.at[it, n_body - 1, mine], (recv1a, recv1b)[it].at[body, me], recv_sem.at[it]
        ).start()

    load_inc.wait()
    for load in load_inv:
        load.wait()
    build(n_body // 2, n_body)
    for k in range(modes):
        real, imag = inc_v[k, 0].astype(F32), inc_v[k, 1].astype(F32)
        cut = [slice(part * h, part * (h + 1)) for h in range(2)]
        value = inverse_product(k, [(real[c], imag[c]) for c in cut], turned=False)
        for h in range(2):
            hold(k, h, value[2 * part * h : 2 * part * (h + 1)])
    for h in range(2):
        rows = density_rows(h)
        for g in range(groups):
            gather(0, h, g, rows)

    pl.semaphore_wait(barrier, n_body + n_mode - 2)
    for off in peers:
        pl.semaphore_signal(
            ready_sem, inc=1, device_id={"mode": lax.rem(me + off, n_mode)}, device_id_type=MESH
        )
    for r in range(n_body - 1):
        post(0, r, x, core)
    pl.semaphore_wait(ready_sem, n_mode - 1)
    for h in range(2):
        for r in range(n_body):
            for dx in across[:-1]:
                post(0, r, lax.rem(x + dx, xdim), h)
        if h == 0:
            for r in range(n_body):
                post(0, r, x, 1 - core)
    keep_own(0)

    load_w.wait()
    for off in peers:
        pltpu.make_async_remote_copy(
            src_ref=w_v, dst_ref=wall.at[me], send_sem=send_sem.at[4], recv_sem=recv_sem.at[6],
            device_id={"mode": lax.rem(me + off, n_mode)}, device_id_type=MESH,
        ).start()
    pltpu.make_async_copy(w_v, wall.at[me], recv_sem.at[6]).start()
    load_near_s.wait()
    load_up.wait()
    load_down.wait()
    load_coup.wait()

    for c in range(2):
        coup_t[c] = jnp.transpose(coup_v[c])

    @pl.loop(0, modes)
    def _(k):
        for c in range(2):
            inv_t[k, c] = jnp.transpose(inv_v[k, c])

    for it in range(ITERS):
        from_body = (recv1a, recv1b)[it]
        arrived(from_body, it)
        modal = []
        for v in range(0, near, 2):
            both = [from_body[near_s[v + j, body]].astype(F32) for j in range(2)]
            modal.append(swap_quadrants(jnp.concatenate(both, 1)).reshape(2 * MODES, 2 * cap))
        modal = jnp.concatenate(modal, 1).astype(BF)
        cycles = jnp.dot(up_v[...], modal, preferred_element_type=F32)
        if it == 0:
            arrived(wall, 6)
        weights = wall[...].astype(F32).reshape(NA, -1)
        scaled = jnp.concatenate([cycles[:NA] * weights, cycles[NA:] * weights], 0).astype(BF)
        back = jnp.dot(down_v[...], scaled, preferred_element_type=F32).astype(BF)
        half = back.shape[0] // 2
        back = jnp.concatenate([back[:half], back[half:]], 1)
        right = coup_t[...].reshape(2 * coup_t.shape[1], -1)
        correction = jnp.dot(back, right, preferred_element_type=F32)
        for j in range(n_mode):
            snd3[it, j] = correction[2 * modes * j : 2 * modes * (j + 1)].astype(BF)
        for off in peers:
            peer = lax.rem(me + off, n_mode)
            pltpu.make_async_remote_copy(
                src_ref=snd3.at[it, peer], dst_ref=recv3.at[it, mine], send_sem=send_sem.at[2 * it + 1],
                recv_sem=recv_sem.at[2 + 2 * it + core], device_id={"mode": peer}, device_id_type=MESH,
            ).start()
        pltpu.make_async_copy(snd3.at[it, me], recv3.at[it, mine], recv_sem.at[2 + 2 * it + core]).start()

        for h in range(2):
            arrived(recv3.at[it, pl.ds(part * h, part)], 2 + 2 * it + h)
            for i in range(part):
                value = recv3[it, part * h + i].astype(F32)
                for q in range(tiles):
                    rbuf[h, q, 2 * modes * i : 2 * modes * (i + 1)] = value[:, 128 * q : 128 * q + 128]
            for k in range(modes):
                sides = []
                for c in range(2):
                    value = [rbuf[h, q, pl.ds(2 * k + c, part, stride=2 * modes), :] for q in range(tiles)]
                    value = jnp.concatenate(value, 1)
                    source = inc_v[k, c].astype(F32)[part * h : part * (h + 1)]
                    sides.append(source - value * (1.0 / NA))
                value = inverse_product(k, [sides])
                if it == ITERS - 1 and h == 1:
                    early = [dbuf[0, q, 2 * part * k : 2 * part * (k + 1)] for q in range(tiles)]
                    early = jnp.concatenate(early, 1)
                    value = [early[:part], value[:part], early[part:], value[part:]]
                    value = jnp.concatenate(value, 0)
                    out_ref[2 * incs * k : 2 * incs * (k + 1)] = value.astype(BF)
                else:
                    hold(k, h, value)
            if it < ITERS - 1:
                rows = density_rows(h)
                for g in range(groups + 1):
                    if g < groups:
                        gather(it + 1, h, g, rows)
                    if g > 0:
                        for r in range((g - 1) * per_group, g * per_group):
                            for dx in across if r < n_body - 1 else across[:-1]:
                                post(it + 1, r, lax.rem(x + dx, xdim), h)
                if h == 1:
                    post(it + 1, n_body - 1, x, 1 - core)
                    keep_own(it + 1)

    for it in range(ITERS):
        sent(snd1.at[it, pl.ds(0, n_body - 1)], 2 * it)
        sent(snd1.at[it, n_body - 1, pl.ds(0, n_mode - 1)], 2 * it)
        sent(snd3.at[it, pl.ds(0, n_mode - 1)], 2 * it + 1)
    sent(wall.at[pl.ds(0, n_mode - 1)], 4)


def solution(mesh):
    n_mode, n_body = mesh.shape["mode"], mesh.shape["body"]
    up, down = tables()

    def local(incident, inverse, coupling, cycle_weight, near_bodies, cycle_nodes, cycle_counts):
        bodies, near = near_bodies.shape
        cap = cycle_nodes.shape[2]
        modes, inc, nodes = incident.shape[1], incident.shape[3], incident.shape[4]
        slots = near * cap
        rows = modes * 2 * inc
        width = 4 * cap
        hbm = pl.BlockSpec(memory_space=pl.ANY)
        out = pl.pallas_call(
            lambda *refs: kernel(n_mode, n_body, *refs),
            out_shape=pltpu.VMEM((rows, nodes), BF),
            in_specs=[hbm] * 9,
            out_specs=pl.BlockSpec(memory_space=pltpu.VMEM),
            scratch_shapes=[
                pltpu.SMEM((near, bodies), jnp.int32),
                pltpu.VMEM((near, bodies), jnp.int32),
                pltpu.VMEM((near, bodies), jnp.int32),
                pltpu.VMEM((near, bodies, cap), jnp.int32),
                pltpu.VMEM((2 * NA, 2 * MODES), BF),
                pltpu.VMEM((4 * MODES, 2 * NA), BF),
                pltpu.VMEM((modes, 2, inc, nodes), BF),
                pltpu.VMEM((NA // n_mode, slots), BF),
                pltpu.VMEM((modes, 2, nodes, nodes), BF),
                pltpu.VMEM((2, nodes, slots), BF),
                pltpu.VMEM((modes, 2, nodes, nodes), BF),
                pltpu.VMEM((2, slots, nodes), BF),
                pltpu.VMEM((bodies, 2 * cap), jnp.int32),
                pltpu.VMEM((bodies * cap // width, nodes, width), BF),
                pltpu.VMEM((2, nodes // 128, rows // 2, 128), F32),
                pltpu.VMEM((2, rows // 2, nodes), F32),
                pltpu.VMEM((ITERS, bodies, n_mode, modes, 2 * cap), BF),
                pltpu.VMEM((bodies, n_mode, modes, 2 * cap), BF),
                pltpu.VMEM((bodies, n_mode, modes, 2 * cap), BF),
                pltpu.VMEM((ITERS, n_mode, 2 * modes, nodes), BF),
                pltpu.VMEM((ITERS, n_mode, 2 * modes, nodes), BF),
                pltpu.VMEM((2, nodes // 128, rows // 2, 128), F32),
                pltpu.VMEM((n_mode, NA // n_mode, slots), BF),
                pltpu.SemaphoreType.DMA((modes + 9,)),
                pltpu.SemaphoreType.DMA((2 * ITERS + 1,)),
                pltpu.SemaphoreType.DMA((3 * ITERS + 1,)),
                pltpu.SemaphoreType.REGULAR,
            ],
            compiler_params=pltpu.CompilerParams(collective_id=0, has_side_effects=True),
            name="sweeps",
        )(
            near_bodies.T, cycle_counts.T, cycle_nodes.transpose(1, 0, 2), jnp.asarray(up), jnp.asarray(down),
            incident[0], cycle_weight[0], inverse[0], coupling[0],
        )
        return out.reshape(1, modes, 2, inc, nodes)

    in_specs = (
        P("body", "mode", None, None, None),
        P("body", "mode", None, None, None),
        P("body", None, None, None),
        P("body", "mode", None),
        P(),
        P(),
        P(),
    )
    out_specs = P("body", "mode", None, None, None)
    return jax.shard_map(local, mesh=mesh, in_specs=in_specs, out_specs=out_specs, check_vma=False)
```

```python
import math

import jax
import jax.numpy as jnp
import numpy as np
from jax import lax
from jax.experimental import pallas as pl
from jax.experimental.pallas import tpu as pltpu
from jax.sharding import PartitionSpec as P

MODES = 32
NA = 256
ITERS = 2
ZDIM = 8
MESH = pl.DeviceIdType.MESH
BF = jnp.bfloat16
F32 = jnp.float32


def tables():
    wavenum = np.arange(MODES) - MODES // 2
    residue = (wavenum[:, None] * np.arange(NA)[None, :]) % NA
    theta = residue.astype(np.float32) * np.float32(2.0 * math.pi / NA)
    cos, sin = np.cos(theta), np.sin(theta)
    up = np.stack([np.stack([cos, sin], -1), np.stack([-sin, cos], -1)], 1)
    up = up.transpose(3, 2, 0, 1).reshape(2 * NA, 2 * MODES)
    down = np.stack([np.stack([cos, sin], 1), np.stack([-sin, cos], 1)], 1)
    turned = np.stack([-down[:, 1], down[:, 0]], 1)
    down = np.concatenate([down.reshape(2 * MODES, 2 * NA), turned.reshape(2 * MODES, 2 * NA)], 0)
    return up.astype(BF), down.astype(BF)


def offsets(bodies):
    ydim = bodies // ZDIM
    far = lambda d, n: min(d, n - d)
    order = [(dy, dz) for dy in range(ydim) for dz in range(ZDIM)]
    order.sort(key=lambda o: (-far(o[0], ydim), -far(o[1], ZDIM), o))
    return order


def target(body, dy, dz, ydim):
    return lax.rem(body // ZDIM + dy, ydim) * ZDIM + lax.rem(lax.rem(body, ZDIM) + dz, ZDIM)


def dot_nt(left, right):
    return lax.dot_general(left, right, (((1,), (1,)), ((), ())), preferred_element_type=F32)


def kernel(
    n_mode, n_body, near_hbm, counts_hbm, nodes_hbm, up_hbm, down_hbm, inc_hbm, w_hbm, inv_hbm, coup_hbm,
    out_ref,
    near_s, near_v, counts_v, nodes_v, up_v, down_v, inc_v, w_v, inv_v, coup_v, inv_t, coup_t,
    picks, onehot, dbuf, dens, snd1, recv1a, recv1b, snd3, recv3, rbuf, wall,
    load_sem, send_sem, recv_sem, ready_sem,
):
    me = lax.axis_index("mode")
    body = lax.axis_index("body")
    xdim = n_mode // 2
    x, core = me // 2, lax.rem(me, 2)
    mine = core * xdim + x
    ydim = n_body // ZDIM
    modes, incs = inv_v.shape[0], inc_v.shape[2]
    part = incs // 2
    near, cap = nodes_v.shape[0], nodes_v.shape[2]
    tiles = rbuf.shape[1]
    order = offsets(n_body)
    across = sorted(range(xdim), key=lambda dx: -min(dx, xdim - dx))
    peers = sorted(range(1, n_mode), key=lambda off: -min(off, n_mode - off))

    pairs = [(inc_hbm, inc_v), (near_hbm, near_v), (counts_hbm, counts_v), (nodes_hbm, nodes_v)]
    pairs += [(inv_hbm.at[k], inv_v.at[k]) for k in range(modes)]
    pairs += [(near_hbm, near_s), (up_hbm, up_v), (down_hbm, down_v), (w_hbm, w_v), (coup_hbm, coup_v)]
    loads = [pltpu.make_async_copy(src, dst, load_sem.at[j]) for j, (src, dst) in enumerate(pairs)]
    load_inc, load_near, load_counts, load_nodes = loads[:4]
    load_inv, (load_near_s, load_up, load_down, load_w, load_coup) = loads[4 : 4 + modes], loads[4 + modes :]

    for load in loads:
        load.start()

    barrier = pltpu.get_barrier_semaphore()
    for dy, dz in order[:-1]:
        pl.semaphore_signal(
            barrier, inc=1, device_id={"body": target(body, dy, dz, ydim)}, device_id_type=MESH
        )
    for off in peers:
        pl.semaphore_signal(
            barrier, inc=1, device_id={"mode": lax.rem(me + off, n_mode)}, device_id_type=MESH
        )

    load_near.wait()
    load_counts.wait()
    load_nodes.wait()
    near_t = jnp.transpose(near_v[...])
    counts_t = jnp.transpose(counts_v[...])
    slot = lax.broadcasted_iota(jnp.int32, (n_body, cap), 1)
    chosen = jnp.full((n_body, cap), -1, jnp.int32)
    for n in range(near):
        ours = jnp.broadcast_to(near_t[:, n : n + 1], (n_body, cap)) == body
        live = slot < jnp.broadcast_to(counts_t[:, n : n + 1], (n_body, cap))
        chosen = jnp.where(ours & live, nodes_v[n], chosen)
    picks[...] = jnp.concatenate([chosen, chosen], 1)

    groups, width = onehot.shape[0], onehot.shape[2]
    per_group = width // cap
    node_index = lax.broadcasted_iota(jnp.int32, (onehot.shape[1], 2 * cap), 0)
    low = lax.broadcasted_iota(jnp.int32, (1, 2 * cap), 1) < cap
    def build(start, stop):
        for r in range(start, stop, 2):
            first, second = (picks[pl.ds(target(body, *order[r + j], ydim), 1), :] for j in range(2))
            row = jnp.where(low, first, second)
            lanes = (r % per_group) * cap
            hit = jnp.where(node_index == row, 1.0, 0.0).astype(BF)
            onehot[r // per_group, :, lanes : lanes + 2 * cap] = hit

    build(0, n_body // 2)

    def arrived(dst, slot):
        pltpu.make_async_copy(dst, dst, recv_sem.at[slot]).wait()

    def sent(block, slot):
        pltpu.make_async_copy(block, block, send_sem.at[slot]).wait()

    def swap_quadrants(block):
        up_half = lax.broadcasted_iota(jnp.int32, block.shape, 1) < modes
        left_half = lax.broadcasted_iota(jnp.int32, block.shape, 2) < cap
        return jnp.where(up_half == left_half, block, pltpu.roll(pltpu.roll(block, modes, 1), cap, 2))

    def inverse_product(k, sides, turned=True):
        first = jnp.concatenate([v for real, imag in sides for v in (real, imag)], 0).astype(BF)
        second = jnp.concatenate([v for real, imag in sides for v in (-imag, real)], 0).astype(BF)
        if turned:
            right = inv_t[k].reshape(2 * inv_t.shape[2], -1)
            return jnp.dot(jnp.concatenate([first, second], 1), right, preferred_element_type=F32)
        return dot_nt(first, inv_v[k, 0]) + dot_nt(second, inv_v[k, 1])

    def hold(k, h, value):
        for q in range(tiles):
            dbuf[h, q, 2 * part * k : 2 * part * (k + 1)] = value[:, 128 * q : 128 * q + 128]

    def density_rows(h):
        for i in range(part):
            rows = [dbuf[h, q, pl.ds(i, 2 * modes, stride=part), :] for q in range(tiles)]
            dens[h, 2 * modes * i : 2 * modes * (i + 1)] = jnp.concatenate(rows, 1)
        return dens[h].astype(BF)

    def gather(it, h, g, rows):
        picked = jnp.dot(rows, onehot[g], preferred_element_type=F32)
        for pair in range(per_group // 2):
            block = picked[:, 128 * pair : 128 * pair + 128].reshape(part, 2 * modes, 2 * cap)
            block = swap_quadrants(block).astype(BF)
            r = g * per_group + 2 * pair
            snd1[it, r, part * h : part * (h + 1)] = block[:, :modes]
            snd1[it, r + 1, part * h : part * (h + 1)] = block[:, modes:]

    def post(it, r, to_x, to_core):
        pltpu.make_async_remote_copy(
            src_ref=snd1.at[it, r, to_core * xdim + to_x], dst_ref=(recv1a, recv1b)[it].at[body, me],
            send_sem=send_sem.at[2 * it], recv_sem=recv_sem.at[it],
            device_id={"mode": 2 * to_x + to_core, "body": target(body, *order[r], ydim)},
            device_id_type=MESH,
        ).start()

    def keep_own(it):
        pltpu.make_async_copy(
            snd1.at[it, n_body - 1, mine], (recv1a, recv1b)[it].at[body, me], recv_sem.at[it]
        ).start()

    load_inc.wait()
    for load in load_inv:
        load.wait()
    build(n_body // 2, n_body)
    for k in range(modes):
        real, imag = inc_v[k, 0].astype(F32), inc_v[k, 1].astype(F32)
        cut = [slice(part * h, part * (h + 1)) for h in range(2)]
        value = inverse_product(k, [(real[c], imag[c]) for c in cut], turned=False)
        for h in range(2):
            hold(k, h, value[2 * part * h : 2 * part * (h + 1)])
    for h in range(2):
        rows = density_rows(h)
        for g in range(groups):
            gather(0, h, g, rows)

    pl.semaphore_wait(barrier, n_body + n_mode - 2)
    for off in peers:
        pl.semaphore_signal(
            ready_sem, inc=1, device_id={"mode": lax.rem(me + off, n_mode)}, device_id_type=MESH
        )
    for r in range(n_body - 1):
        post(0, r, x, core)
    pl.semaphore_wait(ready_sem, n_mode - 1)
    for h in range(2):
        for r in range(n_body):
            for dx in across[:-1]:
                post(0, r, lax.rem(x + dx, xdim), h)
        if h == 0:
            for r in range(n_body):
                post(0, r, x, 1 - core)
    keep_own(0)

    load_w.wait()
    for off in peers:
        pltpu.make_async_remote_copy(
            src_ref=w_v, dst_ref=wall.at[me], send_sem=send_sem.at[4], recv_sem=recv_sem.at[6],
            device_id={"mode": lax.rem(me + off, n_mode)}, device_id_type=MESH,
        ).start()
    pltpu.make_async_copy(w_v, wall.at[me], recv_sem.at[6]).start()
    load_near_s.wait()
    load_up.wait()
    load_down.wait()
    load_coup.wait()

    for c in range(2):
        coup_t[c] = jnp.transpose(coup_v[c])

    @pl.loop(0, modes // 2)
    def _(k):
        for c in range(2):
            inv_t[k, c] = jnp.transpose(inv_v[k, c])

    for it in range(ITERS):
        from_body = (recv1a, recv1b)[it]
        arrived(from_body, it)
        modal = []
        for v in range(0, near, 2):
            both = [from_body[near_s[v + j, body]].astype(F32) for j in range(2)]
            modal.append(swap_quadrants(jnp.concatenate(both, 1)).reshape(2 * MODES, 2 * cap))
        modal = jnp.concatenate(modal, 1).astype(BF)
        cycles = jnp.dot(up_v[...], modal, preferred_element_type=F32)
        if it == 0:
            arrived(wall, 6)
        weights = wall[...].astype(F32).reshape(NA, -1)
        scaled = jnp.concatenate([cycles[:NA] * weights, cycles[NA:] * weights], 0).astype(BF)
        back = jnp.dot(down_v[...], scaled, preferred_element_type=F32).astype(BF)
        half = back.shape[0] // 2
        back = jnp.concatenate([back[:half], back[half:]], 1)
        right = coup_t[...].reshape(2 * coup_t.shape[1], -1)
        correction = jnp.dot(back, right, preferred_element_type=F32)
        for j in range(n_mode):
            snd3[it, j] = correction[2 * modes * j : 2 * modes * (j + 1)].astype(BF)
        for off in peers:
            peer = lax.rem(me + off, n_mode)
            pltpu.make_async_remote_copy(
                src_ref=snd3.at[it, peer], dst_ref=recv3.at[it, mine], send_sem=send_sem.at[2 * it + 1],
                recv_sem=recv_sem.at[2 + 2 * it + core], device_id={"mode": peer}, device_id_type=MESH,
            ).start()
        pltpu.make_async_copy(snd3.at[it, me], recv3.at[it, mine], recv_sem.at[2 + 2 * it + core]).start()

        if it == 0:
            @pl.loop(modes // 2, modes)
            def _(k):
                for c in range(2):
                    inv_t[k, c] = jnp.transpose(inv_v[k, c])

        for h in range(2):
            arrived(recv3.at[it, pl.ds(part * h, part)], 2 + 2 * it + h)
            for i in range(part):
                value = recv3[it, part * h + i].astype(F32)
                for q in range(tiles):
                    rbuf[h, q, 2 * modes * i : 2 * modes * (i + 1)] = value[:, 128 * q : 128 * q + 128]
            for k in range(modes):
                sides = []
                for c in range(2):
                    value = [rbuf[h, q, pl.ds(2 * k + c, part, stride=2 * modes), :] for q in range(tiles)]
                    value = jnp.concatenate(value, 1)
                    source = inc_v[k, c].astype(F32)[part * h : part * (h + 1)]
                    sides.append(source - value * (1.0 / NA))
                value = inverse_product(k, [sides])
                if it == ITERS - 1 and h == 1:
                    early = [dbuf[0, q, 2 * part * k : 2 * part * (k + 1)] for q in range(tiles)]
                    early = jnp.concatenate(early, 1)
                    value = [early[:part], value[:part], early[part:], value[part:]]
                    value = jnp.concatenate(value, 0)
                    out_ref[2 * incs * k : 2 * incs * (k + 1)] = value.astype(BF)
                else:
                    hold(k, h, value)
            if it < ITERS - 1:
                rows = density_rows(h)
                for g in range(groups + 1):
                    if g < groups:
                        gather(it + 1, h, g, rows)
                    if g > 0:
                        for r in range((g - 1) * per_group, g * per_group):
                            for dx in across if r < n_body - 1 else across[:-1]:
                                post(it + 1, r, lax.rem(x + dx, xdim), h)
                if h == 1:
                    post(it + 1, n_body - 1, x, 1 - core)
                    keep_own(it + 1)

    for it in range(ITERS):
        sent(snd1.at[it, pl.ds(0, n_body - 1)], 2 * it)
        sent(snd1.at[it, n_body - 1, pl.ds(0, n_mode - 1)], 2 * it)
        sent(snd3.at[it, pl.ds(0, n_mode - 1)], 2 * it + 1)
    sent(wall.at[pl.ds(0, n_mode - 1)], 4)


def solution(mesh):
    n_mode, n_body = mesh.shape["mode"], mesh.shape["body"]
    up, down = tables()

    def local(incident, inverse, coupling, cycle_weight, near_bodies, cycle_nodes, cycle_counts):
        bodies, near = near_bodies.shape
        cap = cycle_nodes.shape[2]
        modes, inc, nodes = incident.shape[1], incident.shape[3], incident.shape[4]
        slots = near * cap
        rows = modes * 2 * inc
        width = 4 * cap
        hbm = pl.BlockSpec(memory_space=pl.ANY)
        out = pl.pallas_call(
            lambda *refs: kernel(n_mode, n_body, *refs),
            out_shape=pltpu.VMEM((rows, nodes), BF),
            in_specs=[hbm] * 9,
            out_specs=pl.BlockSpec(memory_space=pltpu.VMEM),
            scratch_shapes=[
                pltpu.SMEM((near, bodies), jnp.int32),
                pltpu.VMEM((near, bodies), jnp.int32),
                pltpu.VMEM((near, bodies), jnp.int32),
                pltpu.VMEM((near, bodies, cap), jnp.int32),
                pltpu.VMEM((2 * NA, 2 * MODES), BF),
                pltpu.VMEM((4 * MODES, 2 * NA), BF),
                pltpu.VMEM((modes, 2, inc, nodes), BF),
                pltpu.VMEM((NA // n_mode, slots), BF),
                pltpu.VMEM((modes, 2, nodes, nodes), BF),
                pltpu.VMEM((2, nodes, slots), BF),
                pltpu.VMEM((modes, 2, nodes, nodes), BF),
                pltpu.VMEM((2, slots, nodes), BF),
                pltpu.VMEM((bodies, 2 * cap), jnp.int32),
                pltpu.VMEM((bodies * cap // width, nodes, width), BF),
                pltpu.VMEM((2, nodes // 128, rows // 2, 128), F32),
                pltpu.VMEM((2, rows // 2, nodes), F32),
                pltpu.VMEM((ITERS, bodies, n_mode, modes, 2 * cap), BF),
                pltpu.VMEM((bodies, n_mode, modes, 2 * cap), BF),
                pltpu.VMEM((bodies, n_mode, modes, 2 * cap), BF),
                pltpu.VMEM((ITERS, n_mode, 2 * modes, nodes), BF),
                pltpu.VMEM((ITERS, n_mode, 2 * modes, nodes), BF),
                pltpu.VMEM((2, nodes // 128, rows // 2, 128), F32),
                pltpu.VMEM((n_mode, NA // n_mode, slots), BF),
                pltpu.SemaphoreType.DMA((modes + 9,)),
                pltpu.SemaphoreType.DMA((2 * ITERS + 1,)),
                pltpu.SemaphoreType.DMA((3 * ITERS + 1,)),
                pltpu.SemaphoreType.REGULAR,
            ],
            compiler_params=pltpu.CompilerParams(collective_id=0, has_side_effects=True),
            name="sweeps",
        )(
            near_bodies.T, cycle_counts.T, cycle_nodes.transpose(1, 0, 2), jnp.asarray(up), jnp.asarray(down),
            incident[0], cycle_weight[0], inverse[0], coupling[0],
        )
        return out.reshape(1, modes, 2, inc, nodes)

    in_specs = (
        P("body", "mode", None, None, None),
        P("body", "mode", None, None, None),
        P("body", None, None, None),
        P("body", "mode", None),
        P(),
        P(),
        P(),
    )
    out_specs = P("body", "mode", None, None, None)
    return jax.shard_map(local, mesh=mesh, in_specs=in_specs, out_specs=out_specs, check_vma=False)
```
